512 devices in a mesh: dp: 64 (over z, x, core), head: 8 (over y).
Axes of the slice: x: 4, y: 8, z: 8, core: 2. Of those that a mesh axis runs over, the one named last changes fastest.
Arguments:
- queries: bfloat16 [65536, 2048], P('dp', 'head'), may hold values from -160 to 160
- table: bfloat16 [2048, 128, 768], P('dp', 'head'), may hold values from -6 to 6
- owner: int32 [2048, 1], P('dp'), may hold values from 0 to 63; in each aligned block of 32 rows (0 to 31, 32 to 63, ...) at most 2 rows name the same one
- local_id: int32 [2048, 1], P('dp'), may hold values from 0 to 31
- w_key: bfloat16 [768, 2048], P(None, 'head'), may hold values from -0.21875 to 0.21875
- w_value: bfloat16 [768, 2048], P(None, 'head'), may hold values from -0.21875 to 0.21875
- grad_out: bfloat16 [65536, 2048], P('dp', 'head'), may hold values from -6 to 6
Outputs:
- attended: bfloat16 [65536, 2048], P('dp', 'head')
- grad_key: float32 [768, 2048], P('dp', 'head')
- grad_value: float32 [768, 2048], P('dp', 'head')
The draws below stay inside these ranges and needn't reach their ends.
Inputs may be any that keep to these rules, and one draw needn't show every extreme that they name: Among the 32 slots of one index of dp (aligned blocks of rows) no owner is named more than 2 times, a bound that some block reaches.
All inputs are finite; a program needn't handle non-finite values.
Results may differ from the reference program's by a relative error of at most 0.015.
The reference program's roundings to bfloat16 on the way (of `encoded`, `probs_low`, `grad_scores` and `grad_kv`) count: a program that leaves them out, or rounds other values in their place, can miss the bound.
Values may be sent and summed in bfloat16 or wider, within the bound.
No kernel may reach another device: no remote copies, remote signals or barrier semaphores. Data moves between devices by JAX's collectives and lax.ppermute only.
A program may use at most 64 MiB of HBM per device.

```python
import math
import jax
import jax.numpy as jnp
import numpy as np
from jax import lax

HEADS = 16
HEAD_DIM = 128
ENC = 768
STRETCH = 64
NEIGH_LEN = 128
MOST = 2
CH_DEV = 16
NB_DEV = 32
TOKENS = 65536
SLOTS = 2048
NEIGHBOURS = 2048
N_DP = 64


def draw_queries(key, part):
    first_key = jax.random.fold_in(key, 0)
    values = jnp.clip(jax.random.normal(first_key, (TOKENS, HEADS * HEAD_DIM), jnp.float32), -4.0, 4.0)
    return values.astype(jnp.bfloat16)


def set_ends(drawn, rng, low, largest):
    spot = [jax.random.randint(jax.random.fold_in(rng, axis), (), 0, length) for axis, length in enumerate(drawn.shape)]
    main_axis = drawn.shape.index(max(drawn.shape))
    beside = spot[:main_axis] + [(spot[main_axis] + 1) % drawn.shape[main_axis]] + spot[main_axis + 1:]
    return drawn.at[tuple(spot)].set(low).at[tuple(beside)].set(largest)


def level_of(key, dims, pieces, smallest, high):
    def one(axis_at, shards_of):
        draws = jax.random.uniform(jax.random.fold_in(jax.random.fold_in(key, 6), axis_at), (shards_of,), jnp.float32, smallest / len(pieces), high / len(pieces))
        return jnp.repeat(jnp.exp(draws), dims[axis_at] // shards_of).reshape((-1,) + (1,) * (len(dims) - axis_at - 1))

    loudness = one(*pieces[0])
    for cut in pieces[1:]:
        loudness = loudness * one(*cut)
    return loudness


def cumulative_ranks(amount, slope):
    loads = [(1 << 20) // math.isqrt(rank ** slope) + 1 for rank in range(1, amount + 1)]
    width = 1 + sum(loads) // (1 << 30)
    return np.cumsum(np.array([max(1, weight // width) for weight in loads]))


def skewed_ids(rng, extent, number_of, skew):
    grid = cumulative_ranks(number_of, skew)
    ticket = jax.random.randint(jax.random.fold_in(rng, 1), extent, 0, int(grid[number_of - 1]))
    standing = jnp.searchsorted(jnp.asarray(grid, jnp.int32), ticket, side="right")
    return jax.random.permutation(jax.random.fold_in(rng, 2), number_of)[standing].astype(jnp.int32)


def assign_block(stream_key, own, number, rows, number_of, top, bound, lean):
    sequence = jax.random.permutation(stream_key, number_of)
    packed, usual = portions_of(number_of, rows * top, bound, lean, True), portions_of(number_of, rows * top, bound, lean, False)
    places = jnp.arange(number_of)

    def named(lengths, turn):
        used = int((lengths > 0).sum())
        fixed = max(1, used // 4)
        shifted = fixed + (places - fixed + turn * (used - fixed)) % max(1, number_of - fixed)
        return jnp.zeros((number_of,), jnp.int32).at[sequence[jnp.where(places < fixed, places, shifted)]].set(jnp.asarray(lengths, jnp.int32))

    lengths = jnp.where(number % 4 == 0, named(packed, number // 4), named(usual, number - number // 4 - 1))
    mixed = jax.random.permutation(jax.random.fold_in(own, 3), number_of)
    source_of, taker = mixed[0:number_of // 2 * 2:2], mixed[1:number_of // 2 * 2:2]
    slack = jnp.minimum(lengths[source_of] - 1, bound - lengths[taker]) // 2
    slack = jnp.where((source_of == sequence[0]) | (taker == sequence[0]) | (lengths[taker] == 0), 0, jnp.maximum(slack, 0))
    shifted = jax.random.randint(jax.random.fold_in(own, 4), (number_of // 2,), 0, 1 << 20) % (slack + 1)
    lengths = lengths.at[source_of].add(-shifted).at[taker].add(shifted)
    members = jnp.searchsorted(jnp.cumsum(lengths), jnp.arange(rows * top), side="right").astype(jnp.int32)
    listing = members.reshape(top, rows).T
    listing = listing[jax.random.permutation(jax.random.fold_in(own, 1), rows)]
    turn = jax.random.randint(jax.random.fold_in(own, 2), (rows, 1), 0, top)
    return jnp.take_along_axis(listing, (jnp.arange(top)[None, :] + turn) % top, axis=1)


def portions_of(amount, total, limit, skew, full):
    weights = [(1 << 20) // math.isqrt(standing ** skew) + 1 for standing in range(1, amount + 1)]
    largest = limit if full else min(limit, max(-(-total // amount), total * weights[0] // sum(weights)))
    least = 1 if total - largest >= amount - 1 else 0
    given, rest = [largest] + [least] * (amount - 1), total - largest - least * (amount - 1)
    while rest > 0:
        movable = [i for i in range(1, amount) if given[i] < largest] or [i for i in range(1, amount) if given[i] < limit]
        whole, remaining = sum([weights[i] for i in movable]), rest
        for i in movable:
            addition = min(limit - given[i], max(1, remaining * weights[i] // whole), rest)
            given[i] = given[i] + addition
            rest = rest - addition
    return np.array(given)


def gaussian(own_key, extent, deviation, limit, pieces=(), kind=jnp.bfloat16):
    values = deviation * jax.random.normal(own_key, extent, jnp.float32)
    if pieces:
        values = values * level_of(own_key, extent, pieces, -0.22, 0.18)
    return jnp.clip(values, -limit, limit).astype(kind)


def setup_inputs(seed: int = 0) -> dict:
    keys = jax.random.split(jax.random.key(seed), 8)
    queries = draw_queries(jax.random.fold_in(keys[7], 71), 0)
    table = gaussian(keys[1], (NEIGHBOURS, NEIGH_LEN, ENC), 1.0, 6.0, ((0, 64), (1, 8)))
    owner_keys = jax.random.split(jax.random.fold_in(keys[2], 1), SLOTS // (2 * CH_DEV))
    owner_turns = jax.random.permutation(jax.random.fold_in(keys[2], 3), SLOTS // (2 * CH_DEV))
    owner = jax.vmap(lambda own, number: assign_block(jax.random.fold_in(keys[2], 2), own, number, 2 * CH_DEV, N_DP, 1, MOST, 2))(owner_keys, owner_turns).reshape((SLOTS, 1))
    local_id = set_ends(skewed_ids(keys[3], (SLOTS, 1), NB_DEV, 2), jax.random.fold_in(keys[3], 3), 0, NB_DEV - 1).astype(jnp.int32)
    w_key = gaussian(keys[4], (ENC, HEADS * HEAD_DIM), ENC ** -0.5, 0.21875, ((1, 8),))
    w_value = gaussian(keys[5], (ENC, HEADS * HEAD_DIM), ENC ** -0.5, 0.21875, ((1, 8),))
    grad_out = gaussian(keys[6], (TOKENS, HEADS * HEAD_DIM), 1.0, 6.0, ((0, 64), (1, 8)))
    return {"queries": queries, "table": table, "owner": owner, "local_id": local_id, "w_key": w_key, "w_value": w_value, "grad_out": grad_out}


def reference(queries, table, owner, local_id, w_key, w_value, grad_out):
    score_scale = HEAD_DIM ** -0.5
    full_width = HEADS * HEAD_DIM
    w_both = jnp.concatenate([w_key, w_value], axis=1)
    neighbour = (owner[:, 0] * NB_DEV + local_id[:, 0]).astype(jnp.int32)
    block_slots = 2 * CH_DEV
    block_tokens = CH_DEV * STRETCH

    def one_block(running, index):
        picked = lax.dynamic_slice_in_dim(neighbour, (index * block_slots).astype(jnp.int32), block_slots)
        encoded = jnp.take(table, picked, axis=0).reshape(-1, ENC)
        key_values = jnp.dot(encoded, w_both, preferred_element_type=jnp.float32).astype(jnp.bfloat16)
        paired = key_values.reshape(CH_DEV, 2 * NEIGH_LEN, 2, HEADS, HEAD_DIM).astype(jnp.float32)
        key_rows = paired[:, :, 0]
        value_rows = paired[:, :, 1]
        first = (index * block_tokens).astype(jnp.int32)
        query_rows = lax.dynamic_slice_in_dim(queries, first, block_tokens).reshape(CH_DEV, STRETCH, HEADS, HEAD_DIM).astype(jnp.float32)
        upstream = lax.dynamic_slice_in_dim(grad_out, first, block_tokens).reshape(CH_DEV, STRETCH, HEADS, HEAD_DIM).astype(jnp.float32)
        scores = jnp.einsum("cqhd,ckhd->chqk", query_rows, key_rows) * score_scale
        row_max = jnp.max(scores, axis=-1, keepdims=True)
        weights = jnp.exp(scores - row_max)
        probs_high = weights / jnp.sum(weights, axis=-1, keepdims=True)
        probs_low = probs_high.astype(jnp.bfloat16).astype(jnp.float32)
        attended = jnp.einsum("chqk,ckhd->cqhd", probs_low, value_rows).astype(jnp.bfloat16)
        grad_values = jnp.einsum("chqk,cqhd->ckhd", probs_low, upstream)
        grad_probs = jnp.einsum("cqhd,ckhd->chqk", upstream, value_rows)
        row_inner = jnp.sum(probs_high * grad_probs, axis=-1, keepdims=True)
        grad_scores = (probs_high * (grad_probs - row_inner)).astype(jnp.bfloat16).astype(jnp.float32)
        grad_keys = jnp.einsum("chqk,cqhd->ckhd", grad_scores, query_rows) * score_scale
        grad_kv = jnp.stack([grad_keys, grad_values], axis=2).astype(jnp.bfloat16).reshape(-1, 2 * full_width)
        running = running + jnp.dot(encoded.T, grad_kv, preferred_element_type=jnp.float32)
        return running, attended.reshape(block_tokens, full_width)

    initial = jnp.zeros((ENC, 2 * full_width), jnp.float32)
    summed, blocks = lax.scan(one_block, initial, jnp.arange(N_DP, dtype=jnp.int32))
    attended = blocks.reshape(TOKENS, full_width)
    return attended, summed[:, :full_width], summed[:, full_width:]
```

```python
import functools

import jax
import jax.numpy as jnp
from jax import lax
from jax.experimental import pallas as pl
from jax.experimental.pallas import tpu as pltpu
from jax.sharding import PartitionSpec as P

HEAD_DIM = 128
STRETCH = 64
MOST = 2
CHUNKS = 2
GROUP = 4


def block_diagonal(rows):
    left, right = rows[:, :HEAD_DIM], rows[:, HEAD_DIM:]
    zero = jnp.zeros_like(left)
    return jnp.concatenate(
        [jnp.concatenate([left, zero], axis=1), jnp.concatenate([zero, right], axis=1)], axis=0
    )


def dot_nt(a, b):
    return lax.dot_general(a, b, (((1,), (1,)), ((), ())), preferred_element_type=jnp.float32)


def dot_tn(a, b):
    return lax.dot_general(a, b, (((0,), (0,)), ((), ())), preferred_element_type=jnp.float32)


def attention_kernel(*refs, pieces, rows):
    q_ref, g_ref, wk_ref, wv_ref = refs[:4]
    e_refs = refs[4 : 4 + pieces]
    att_ref, grad_ref, kv_ref, dkv_ref, acc_ref = refs[4 + pieces :]
    step = pl.program_id(0)
    width = wk_ref.shape[1]
    score_scale = HEAD_DIM ** (-0.5)
    encoded = jnp.concatenate([e[...] for e in e_refs], axis=0)
    kv_ref[:, :, :width] = (
        jnp.dot(encoded, wk_ref[...], preferred_element_type=jnp.float32)
        .astype(jnp.bfloat16)
        .reshape(pieces, GROUP * rows, width)
    )
    kv_ref[:, :, width:] = (
        jnp.dot(encoded, wv_ref[...], preferred_element_type=jnp.float32)
        .astype(jnp.bfloat16)
        .reshape(pieces, GROUP * rows, width)
    )
    keys_total = pieces * rows
    for s in range(GROUP):
        kv = kv_ref[:, s * rows : (s + 1) * rows, :].reshape(keys_total, 2 * width)
        k, v = kv[:, :width], kv[:, width:]
        q2 = block_diagonal(q_ref[s * STRETCH : (s + 1) * STRETCH, :])
        g2 = block_diagonal(g_ref[s * STRETCH : (s + 1) * STRETCH, :])
        scores = dot_nt(q2, k) * score_scale
        weights = jnp.exp(scores - jnp.max(scores, axis=1, keepdims=True))
        probs = weights * (1.0 / jnp.sum(weights, axis=1, keepdims=True))
        probs_low = probs.astype(jnp.bfloat16)
        out2 = jnp.dot(probs_low, v, preferred_element_type=jnp.float32)
        att_ref[s * STRETCH : (s + 1) * STRETCH, :] = jnp.concatenate(
            [out2[:STRETCH, :HEAD_DIM], out2[STRETCH:, HEAD_DIM:]], axis=1
        ).astype(jnp.bfloat16)
        grad_probs = dot_nt(g2, v)
        inner = jnp.sum(probs * grad_probs, axis=1, keepdims=True)
        grad_scores = (probs * (grad_probs - inner)).astype(jnp.bfloat16)
        cols = slice(s * keys_total, (s + 1) * keys_total)
        dkv_ref[:width, cols] = (dot_tn(q2, grad_scores) * score_scale).astype(jnp.bfloat16)
        dkv_ref[width:, cols] = dot_tn(g2, probs_low).astype(jnp.bfloat16)
    by_stretch = jnp.concatenate(
        [e[s * rows : (s + 1) * rows, :] for s in range(GROUP) for e in e_refs], axis=0
    )
    part = jnp.dot(dkv_ref[...], by_stretch, preferred_element_type=jnp.float32)

    @pl.when(step == 0)
    def _():
        acc_ref[...] = part

    @pl.when(step > 0)
    def _():
        acc_ref[...] += part

    @pl.when(step == pl.num_programs(0) - 1)
    def _():
        grad_ref[...] = acc_ref[...].T.astype(grad_ref.dtype)


def attend(queries, grad_out, w_key, w_value, encoded):
    tokens, width = queries.shape
    enc = w_key.shape[0]
    stretches = tokens // STRETCH
    pieces = len(encoded)
    rows = encoded[0].shape[0] // stretches
    keys_total = pieces * rows
    steps = stretches // GROUP
    token_block = pl.BlockSpec((GROUP * STRETCH, width), lambda i: (i, 0))
    whole_w = pl.BlockSpec((enc, width), lambda i: (0, 0))
    piece_block = pl.BlockSpec((GROUP * rows, enc), lambda i: (i, 0))
    all_keys = stretches * keys_total
    flops = 2 * all_keys * enc * 4 * width + 10 * tokens * keys_total * width
    return pl.pallas_call(
        functools.partial(attention_kernel, pieces=pieces, rows=rows),
        grid=(steps,),
        in_specs=[token_block, token_block, whole_w, whole_w] + [piece_block] * pieces,
        out_specs=[token_block, pl.BlockSpec((enc, 2 * width), lambda i: (0, 0))],
        out_shape=[
            jax.ShapeDtypeStruct((tokens, width), jnp.bfloat16),
            jax.ShapeDtypeStruct((enc, 2 * width), jnp.bfloat16),
        ],
        scratch_shapes=[
            pltpu.VMEM((pieces, GROUP * rows, 2 * width), jnp.bfloat16),
            pltpu.VMEM((2 * width, GROUP * keys_total), jnp.bfloat16),
            pltpu.VMEM((2 * width, enc), jnp.float32),
        ],
        cost_estimate=pl.CostEstimate(flops=flops, bytes_accessed=10_000_000, transcendentals=1_000_000),
        compiler_params=pltpu.CompilerParams(vmem_limit_bytes=48 * 1024 * 1024),
        name="attention",
    )(queries, grad_out, w_key, w_value, *encoded)


def slot_ranks(owners):
    slot_count = owners.shape[0]
    row_order = lax.broadcasted_iota(jnp.int32, (slot_count, slot_count), 0)
    col_order = lax.broadcasted_iota(jnp.int32, (slot_count, slot_count), 1)
    same_owner = (owners[:, None] == owners[None, :]) & (row_order < col_order)
    return jnp.sum(same_owner.astype(jnp.int32), axis=0)


def exchange(x):
    return lax.all_to_all(x, "dp", split_axis=0, concat_axis=0, tiled=True)


def ring_gather(x, far_right):
    size = lax.axis_size("head")
    rightward = [(i, (i + 1) % size) for i in range(size)]
    leftward = [(i, (i - 1) % size) for i in range(size)]
    pieces = [x]
    right = left = x
    for _ in range((size - 1) // 2):
        right = lax.ppermute(right, "head", rightward)
        left = lax.ppermute(left, "head", leftward)
        pieces += [right, left]
    if far_right:
        pieces.append(lax.ppermute(right, "head", rightward))
    else:
        pieces.append(lax.ppermute(left, "head", leftward))
    return pieces


def per_device(queries, table, owner, local_id, w_key, w_value, grad_out):
    groups = lax.axis_size("dp")
    owners = owner[:, 0]
    slot_ids = local_id[:, 0]
    slot_count = owners.shape[0]
    slot_rank = slot_ranks(owners)
    pick_index = lax.broadcasted_iota(jnp.int32, (1, 1, MOST), 2)
    owner_index = lax.broadcasted_iota(jnp.int32, (1, groups, 1), 1)
    chosen = (owners[:, None, None] == owner_index) & (slot_rank[:, None, None] == pick_index)
    wanted = jnp.sum(jnp.where(chosen, slot_ids[:, None, None], 0), axis=0)
    asked_ids = exchange(wanted).reshape(-1)
    neighbours, part, enc_width = table.shape
    rows = part // CHUNKS
    cut_table = table.reshape(neighbours * CHUNKS, rows, enc_width)
    own_index = owners * MOST + slot_rank
    pieces = []
    for chunk in range(CHUNKS):
        replies = jnp.take(cut_table, asked_ids * CHUNKS + chunk, axis=0, mode="clip")
        fetched = exchange(replies.reshape(groups, MOST, rows, enc_width))
        if pieces:
            fetched, pieces = lax.optimization_barrier((fetched, pieces))
        fetched = fetched.reshape(groups * MOST, rows, enc_width)
        own = jnp.take(fetched, own_index, axis=0, mode="clip")
        pieces += ring_gather(own.reshape(slot_count * rows, enc_width), chunk % 2 == 0)
    attended, grads = attend(queries, grad_out, w_key, w_value, pieces)
    width = w_key.shape[1]
    share = enc_width // groups
    lanes = 2 * width // 128
    sent = grads.reshape(groups, share, lanes, 128).transpose(0, 2, 1, 3)
    terms = exchange(sent.reshape(groups, lanes * share, 128))
    total = jnp.sum(terms.astype(jnp.float32), axis=0).reshape(lanes, share, 128)
    total = total.transpose(1, 0, 2).reshape(share, 2 * width)
    return attended, total[:, :width], total[:, width:]


def solution(mesh):
    in_specs = (
        P("dp", "head"),
        P("dp", "head", None),
        P("dp", None),
        P("dp", None),
        P(None, "head"),
        P(None, "head"),
        P("dp", "head"),
    )
    out_specs = (P("dp", "head"), P("dp", "head"), P("dp", "head"))
    return jax.shard_map(
        per_device, mesh=mesh, in_specs=in_specs, out_specs=out_specs, check_vma=False
    )
```

```python
import functools

import jax
import jax.numpy as jnp
from jax import lax
from jax.experimental import pallas as pl
from jax.experimental.pallas import tpu as pltpu
from jax.sharding import PartitionSpec as P

HEAD_DIM = 128
STRETCH = 64
MOST = 2
CHUNKS = 2
CORES = 2
GROUP = 4


def block_diagonal(rows):
    left, right = rows[:, :HEAD_DIM], rows[:, HEAD_DIM:]
    zero = jnp.zeros_like(left)
    return jnp.concatenate(
        [jnp.concatenate([left, zero], axis=1), jnp.concatenate([zero, right], axis=1)], axis=0
    )


def dot_nt(a, b):
    return lax.dot_general(a, b, (((1,), (1,)), ((), ())), preferred_element_type=jnp.float32)


def dot_tn(a, b):
    return lax.dot_general(a, b, (((0,), (0,)), ((), ())), preferred_element_type=jnp.float32)


def attention_kernel(*refs, pieces, rows):
    q_ref, g_ref, wk_ref, wv_ref = refs[:4]
    e_refs = refs[4 : 4 + pieces]
    att_ref, grad_ref, kv_ref, dkv_ref, acc_ref = refs[4 + pieces :]
    step = pl.program_id(0)
    width = wk_ref.shape[1]
    score_scale = HEAD_DIM ** (-0.5)
    encoded = jnp.concatenate([e[...] for e in e_refs], axis=0)
    kv_ref[:, :, :width] = (
        jnp.dot(encoded, wk_ref[...], preferred_element_type=jnp.float32)
        .astype(jnp.bfloat16)
        .reshape(pieces, GROUP * rows, width)
    )
    kv_ref[:, :, width:] = (
        jnp.dot(encoded, wv_ref[...], preferred_element_type=jnp.float32)
        .astype(jnp.bfloat16)
        .reshape(pieces, GROUP * rows, width)
    )
    keys_total = pieces * rows
    for s in range(GROUP):
        kv = kv_ref[:, s * rows : (s + 1) * rows, :].reshape(keys_total, 2 * width)
        k, v = kv[:, :width], kv[:, width:]
        q2 = block_diagonal(q_ref[s * STRETCH : (s + 1) * STRETCH, :])
        g2 = block_diagonal(g_ref[s * STRETCH : (s + 1) * STRETCH, :])
        scores = dot_nt(q2, k) * score_scale
        weights = jnp.exp(scores - jnp.max(scores, axis=1, keepdims=True))
        probs = weights * (1.0 / jnp.sum(weights, axis=1, keepdims=True))
        probs_low = probs.astype(jnp.bfloat16)
        out2 = jnp.dot(probs_low, v, preferred_element_type=jnp.float32)
        att_ref[s * STRETCH : (s + 1) * STRETCH, :] = jnp.concatenate(
            [out2[:STRETCH, :HEAD_DIM], out2[STRETCH:, HEAD_DIM:]], axis=1
        ).astype(jnp.bfloat16)
        grad_probs = dot_nt(g2, v)
        inner = jnp.sum(probs * grad_probs, axis=1, keepdims=True)
        grad_scores = (probs * (grad_probs - inner)).astype(jnp.bfloat16)
        cols = slice(s * keys_total, (s + 1) * keys_total)
        dkv_ref[:width, cols] = (dot_tn(q2, grad_scores) * score_scale).astype(jnp.bfloat16)
        dkv_ref[width:, cols] = dot_tn(g2, probs_low).astype(jnp.bfloat16)
    by_stretch = jnp.concatenate(
        [e[s * rows : (s + 1) * rows, :] for s in range(GROUP) for e in e_refs], axis=0
    )
    part = jnp.dot(dkv_ref[...], by_stretch, preferred_element_type=jnp.float32)

    @pl.when(step == 0)
    def _():
        acc_ref[...] = part

    @pl.when(step > 0)
    def _():
        acc_ref[...] += part

    @pl.when(step == pl.num_programs(0) - 1)
    def _():
        grad_ref[...] = acc_ref[...].T.astype(grad_ref.dtype)


def attend(queries, grad_out, w_key, w_value, encoded):
    tokens, width = queries.shape
    enc = w_key.shape[0]
    stretches = tokens // STRETCH
    pieces = len(encoded)
    rows = encoded[0].shape[0] // stretches
    keys_total = pieces * rows
    steps = stretches // GROUP
    token_block = pl.BlockSpec((GROUP * STRETCH, width), lambda i: (i, 0))
    whole_w = pl.BlockSpec((enc, width), lambda i: (0, 0))
    piece_block = pl.BlockSpec((GROUP * rows, enc), lambda i: (i, 0))
    all_keys = stretches * keys_total
    flops = 2 * all_keys * enc * 4 * width + 10 * tokens * keys_total * width
    return pl.pallas_call(
        functools.partial(attention_kernel, pieces=pieces, rows=rows),
        grid=(steps,),
        in_specs=[token_block, token_block, whole_w, whole_w] + [piece_block] * pieces,
        out_specs=[token_block, pl.BlockSpec((enc, 2 * width), lambda i: (0, 0))],
        out_shape=[
            jax.ShapeDtypeStruct((tokens, width), jnp.bfloat16),
            jax.ShapeDtypeStruct((enc, 2 * width), jnp.bfloat16),
        ],
        scratch_shapes=[
            pltpu.VMEM((pieces, GROUP * rows, 2 * width), jnp.bfloat16),
            pltpu.VMEM((2 * width, GROUP * keys_total), jnp.bfloat16),
            pltpu.VMEM((2 * width, enc), jnp.float32),
        ],
        cost_estimate=pl.CostEstimate(flops=flops, bytes_accessed=10_000_000, transcendentals=1_000_000),
        compiler_params=pltpu.CompilerParams(vmem_limit_bytes=48 * 1024 * 1024),
        name="attention",
    )(queries, grad_out, w_key, w_value, *encoded)


def slot_ranks(owners):
    slot_count = owners.shape[0]
    row_order = lax.broadcasted_iota(jnp.int32, (slot_count, slot_count), 0)
    col_order = lax.broadcasted_iota(jnp.int32, (slot_count, slot_count), 1)
    same_owner = (owners[:, None] == owners[None, :]) & (row_order < col_order)
    return jnp.sum(same_owner.astype(jnp.int32), axis=0)


def exchange(x):
    return lax.all_to_all(x, "dp", split_axis=0, concat_axis=0, tiled=True)


def ring_gather(x, far_right):
    size = lax.axis_size("head")
    rightward = [(i, (i + 1) % size) for i in range(size)]
    leftward = [(i, (i - 1) % size) for i in range(size)]
    pieces = [x]
    right = left = x
    for _ in range((size - 1) // 2):
        right = lax.ppermute(right, "head", rightward)
        left = lax.ppermute(left, "head", leftward)
        pieces += [right, left]
    if far_right:
        pieces.append(lax.ppermute(right, "head", rightward))
    else:
        pieces.append(lax.ppermute(left, "head", leftward))
    return pieces


def per_device(queries, table, owner, local_id, w_key, w_value, grad_out):
    groups = lax.axis_size("dp")
    owners = owner[:, 0]
    slot_ids = local_id[:, 0]
    slot_count = owners.shape[0]
    slot_rank = slot_ranks(owners)
    pick_index = lax.broadcasted_iota(jnp.int32, (1, 1, MOST), 2)
    owner_index = lax.broadcasted_iota(jnp.int32, (1, groups, 1), 1)
    chosen = (owners[:, None, None] == owner_index) & (slot_rank[:, None, None] == pick_index)
    wanted = jnp.sum(jnp.where(chosen, slot_ids[:, None, None], 0), axis=0)
    asked_ids = exchange(wanted).reshape(-1)
    neighbours, part, enc_width = table.shape
    rows = part // CHUNKS
    cut_table = table.reshape(neighbours * CHUNKS, rows, enc_width)
    own_index = owners * MOST + slot_rank
    pieces = []
    for chunk in range(CHUNKS):
        replies = jnp.take(cut_table, asked_ids * CHUNKS + chunk, axis=0, mode="clip")
        fetched = exchange(replies.reshape(groups, MOST, rows, enc_width))
        if pieces:
            fetched, pieces[:-1] = lax.optimization_barrier((fetched, pieces[:-1]))
        fetched = fetched.reshape(groups * MOST, rows, enc_width)
        own = jnp.take(fetched, own_index, axis=0, mode="clip")
        pieces += ring_gather(own.reshape(slot_count * rows, enc_width), chunk % 2 == 0)
    pieces = [pltpu.with_memory_space_constraint(piece, pltpu.HBM) for piece in pieces]
    attended, grads = attend(queries, grad_out, w_key, w_value, pieces)
    width = w_key.shape[1]
    share = enc_width // groups
    lanes = 2 * width // 128
    sent = grads.reshape(groups // CORES, CORES, share, lanes, 128).transpose(1, 0, 3, 2, 4)
    sent = sent.reshape(CORES, groups // CORES, lanes * share, 128)
    core = lax.axis_index("dp") % CORES
    mine = lax.dynamic_index_in_dim(sent, core, 0, keepdims=False)
    partner = lax.dynamic_index_in_dim(sent, 1 - core, 0, keepdims=False)
    swap = [(i, i ^ 1) for i in range(groups)]
    both = mine.astype(jnp.float32) + lax.ppermute(partner, "dp", swap).astype(jnp.float32)
    same_core = [list(range(c, groups, CORES)) for c in range(CORES)]
    terms = lax.all_to_all(
        both.astype(jnp.bfloat16),
        "dp",
        split_axis=0,
        concat_axis=0,
        axis_index_groups=same_core,
        tiled=True,
    )
    total = jnp.sum(terms.astype(jnp.float32), axis=0).reshape(lanes, share, 128)
    total = total.transpose(1, 0, 2).reshape(share, 2 * width)
    return attended, total[:, :width], total[:, width:]


def solution(mesh):
    in_specs = (
        P("dp", "head"),
        P("dp", "head", None),
        P("dp", None),
        P("dp", None),
        P(None, "head"),
        P(None, "head"),
        P("dp", "head"),
    )
    out_specs = (P("dp", "head"), P("dp", "head"), P("dp", "head"))
    return jax.shard_map(
        per_device, mesh=mesh, in_specs=in_specs, out_specs=out_specs, check_vma=False
    )
```

```python
import functools

import jax
import jax.numpy as jnp
from jax import lax
from jax.experimental import pallas as pl
from jax.experimental.pallas import tpu as pltpu
from jax.sharding import PartitionSpec as P

HEAD_DIM = 128
STRETCH = 64
MOST = 2
CHUNK_COLS = (512, 256)
CORES = 2
GROUP = 8


def block_diagonal(rows):
    left, right = rows[:, :HEAD_DIM], rows[:, HEAD_DIM:]
    zero = jnp.zeros_like(left)
    return jnp.concatenate(
        [jnp.concatenate([left, zero], axis=1), jnp.concatenate([zero, right], axis=1)], axis=0
    )


def dot_nt(a, b):
    return lax.dot_general(a, b, (((1,), (1,)), ((), ())), preferred_element_type=jnp.float32)


def dot_tn(a, b):
    return lax.dot_general(a, b, (((0,), (0,)), ((), ())), preferred_element_type=jnp.float32)


def full_width(refs, rows):
    return jnp.concatenate([ref[rows, :] for ref in refs], axis=1)


def attention_kernel(*refs, chunks, pieces, rows):
    q_ref, g_ref, wk_ref, wv_ref = refs[:4]
    e_refs = [refs[4 + p : 4 + chunks * pieces : pieces] for p in range(pieces)]
    att_ref, grad_ref, kv_ref, dkv_ref, acc_ref = refs[4 + chunks * pieces :]
    step = pl.program_id(0)
    width = wk_ref.shape[1]
    score_scale = HEAD_DIM ** (-0.5)
    encoded = jnp.concatenate([full_width(e, slice(None)) for e in e_refs], axis=0)
    w_both = jnp.concatenate([wk_ref[...], wv_ref[...]], axis=1)
    kv_ref[...] = (
        jnp.dot(encoded, w_both, preferred_element_type=jnp.float32)
        .astype(jnp.bfloat16)
        .reshape(pieces, GROUP * rows, 2 * width)
    )
    keys_total = pieces * rows
    group = range(GROUP)
    tokens = [slice(s * STRETCH, (s + 1) * STRETCH) for s in group]
    q2 = [block_diagonal(q_ref[tokens[s], :]) for s in group]
    g2 = [block_diagonal(g_ref[tokens[s], :]) for s in group]
    kv = [
        kv_ref[:, s * rows : (s + 1) * rows, :].reshape(keys_total, 2 * width) for s in group
    ]
    scores = [dot_nt(kv[s][:, :width], q2[s]) * score_scale for s in group]
    grad_probs = [dot_nt(kv[s][:, width:], g2[s]) for s in group]
    weights = [jnp.exp(x - jnp.max(x, axis=0, keepdims=True)) for x in scores]
    probs = [x * (1.0 / jnp.sum(x, axis=0, keepdims=True)) for x in weights]
    probs_low = [x.astype(jnp.bfloat16) for x in probs]
    inner = [jnp.sum(p * g, axis=0, keepdims=True) for p, g in zip(probs, grad_probs)]
    grad_scores = [
        (p * (g - i)).astype(jnp.bfloat16) for p, g, i in zip(probs, grad_probs, inner)
    ]
    for s in group:
        out2 = dot_tn(probs_low[s], kv[s][:, width:])
        att_ref[tokens[s], :] = jnp.concatenate(
            [out2[:STRETCH, :HEAD_DIM], out2[STRETCH:, HEAD_DIM:]], axis=1
        ).astype(jnp.bfloat16)
        cols = slice(s * keys_total, (s + 1) * keys_total)
        dkv_ref[:width, cols] = (dot_nt(q2[s].T, grad_scores[s]) * score_scale).astype(jnp.bfloat16)
        dkv_ref[width:, cols] = dot_nt(g2[s].T, probs_low[s]).astype(jnp.bfloat16)
    by_stretch = jnp.concatenate(
        [full_width(e, slice(s * rows, (s + 1) * rows)) for s in group for e in e_refs], axis=0
    )
    part = jnp.dot(dkv_ref[...], by_stretch, preferred_element_type=jnp.float32)

    @pl.when(step == 0)
    def _():
        acc_ref[...] = part

    @pl.when(step > 0)
    def _():
        acc_ref[...] += part

    @pl.when(step == pl.num_programs(0) - 1)
    def _():
        grad_ref[...] = acc_ref[...].T.astype(grad_ref.dtype)


def attend(queries, grad_out, w_key, w_value, encoded):
    tokens, width = queries.shape
    enc = w_key.shape[0]
    stretches = tokens // STRETCH
    pieces = len(encoded[0])
    rows = encoded[0][0].shape[0] // stretches
    keys_total = pieces * rows
    token_block = pl.BlockSpec((GROUP * STRETCH, width), lambda i: (i, 0))
    whole_w = pl.BlockSpec((enc, width), lambda i: (0, 0))
    flat = [piece for chunk in encoded for piece in chunk]
    piece_blocks = [pl.BlockSpec((GROUP * rows, p.shape[1]), lambda i: (i, 0)) for p in flat]
    flops = 2 * stretches * keys_total * enc * 4 * width + 10 * tokens * keys_total * width
    return pl.pallas_call(
        functools.partial(attention_kernel, chunks=len(encoded), pieces=pieces, rows=rows),
        grid=(stretches // GROUP,),
        in_specs=[token_block, token_block, whole_w, whole_w] + piece_blocks,
        out_specs=[token_block, pl.BlockSpec((enc, 2 * width), lambda i: (0, 0))],
        out_shape=[
            jax.ShapeDtypeStruct((tokens, width), jnp.bfloat16),
            jax.ShapeDtypeStruct((enc, 2 * width), jnp.bfloat16),
        ],
        scratch_shapes=[
            pltpu.VMEM((pieces, GROUP * rows, 2 * width), jnp.bfloat16),
            pltpu.VMEM((2 * width, GROUP * keys_total), jnp.bfloat16),
            pltpu.VMEM((2 * width, enc), jnp.float32),
        ],
        cost_estimate=pl.CostEstimate(
            flops=flops, bytes_accessed=10_000_000, transcendentals=1_000_000
        ),
        compiler_params=pltpu.CompilerParams(vmem_limit_bytes=48 * 1024 * 1024),
        name="attention",
    )(queries, grad_out, w_key, w_value, *flat)


def pick_kernel(index_ref, source_ref, out_ref, sem, *, first):
    width = out_ref.shape[2]

    @pl.loop(0, out_ref.shape[0])
    def _(i):
        window = source_ref.at[index_ref[i], :, pl.ds(first, width)]
        pltpu.make_async_copy(window, out_ref.at[i], sem).start()

    pltpu.make_async_copy(out_ref, out_ref, sem).wait()


def pick(source, index, first, width, source_space, out_space, vmem_limit=None):
    count, rows = index.shape[0], source.shape[1]
    return pl.pallas_call(
        functools.partial(pick_kernel, first=first),
        grid_spec=pltpu.PrefetchScalarGridSpec(
            num_scalar_prefetch=1,
            grid=(),
            in_specs=[pl.BlockSpec(memory_space=source_space)],
            out_specs=pl.BlockSpec(memory_space=out_space),
            scratch_shapes=[pltpu.SemaphoreType.DMA],
        ),
        out_shape=jax.ShapeDtypeStruct((count, rows, width), source.dtype),
        cost_estimate=pl.CostEstimate(
            flops=0, bytes_accessed=4 * count * rows * width, transcendentals=0
        ),
        compiler_params=pltpu.CompilerParams(vmem_limit_bytes=vmem_limit),
        name="pick",
    )(index, source)


def slot_ranks(owners):
    slot_count = owners.shape[0]
    row_order = lax.broadcasted_iota(jnp.int32, (slot_count, slot_count), 0)
    col_order = lax.broadcasted_iota(jnp.int32, (slot_count, slot_count), 1)
    same_owner = (owners[:, None] == owners[None, :]) & (row_order < col_order)
    return jnp.sum(same_owner.astype(jnp.int32), axis=0)


def exchange(x):
    return lax.all_to_all(x, "dp", split_axis=0, concat_axis=0, tiled=True)


def ring_gather(x, far_right):
    size = lax.axis_size("head")
    rightward = [(i, (i + 1) % size) for i in range(size)]
    leftward = [(i, (i - 1) % size) for i in range(size)]
    pieces = [x]
    right = left = x
    for _ in range((size - 1) // 2):
        right = lax.ppermute(right, "head", rightward)
        left = lax.ppermute(left, "head", leftward)
        pieces += [right, left]
    if far_right:
        pieces.append(lax.ppermute(right, "head", rightward))
    else:
        pieces.append(lax.ppermute(left, "head", leftward))
    return pieces


def per_device(queries, table, owner, local_id, w_key, w_value, grad_out):
    groups = lax.axis_size("dp")
    owners = owner[:, 0]
    slot_ids = local_id[:, 0]
    slot_count = owners.shape[0]
    slot_rank = slot_ranks(owners)
    pick_index = lax.broadcasted_iota(jnp.int32, (1, 1, MOST), 2)
    owner_index = lax.broadcasted_iota(jnp.int32, (1, groups, 1), 1)
    chosen = (owners[:, None, None] == owner_index) & (slot_rank[:, None, None] == pick_index)
    wanted = jnp.sum(jnp.where(chosen, slot_ids[:, None, None], 0), axis=0)
    asked_ids = exchange(wanted).reshape(-1)
    part, enc_width = table.shape[1:]
    own_index = owners * MOST + slot_rank
    encoded = []
    first = 0
    for cols in CHUNK_COLS:
        replies = pick(table, asked_ids, first, cols, pltpu.VMEM, pltpu.HBM)
        fetched = exchange(replies.reshape(groups, MOST, part, cols))
        if encoded:
            last = encoded[-1]
            fetched, last[:-1] = lax.optimization_barrier((fetched, last[:-1]))
        fetched = fetched.reshape(groups * MOST, part, cols)
        own = pick(fetched, own_index, 0, cols, pl.ANY, pl.ANY, 1024 * 1024)
        encoded.append(ring_gather(own.reshape(slot_count * part, cols), not encoded))
        first += cols
    encoded = [
        [pltpu.with_memory_space_constraint(piece, pltpu.HBM) for piece in chunk]
        for chunk in encoded
    ]
    attended, grads = attend(queries, grad_out, w_key, w_value, encoded)
    width = w_key.shape[1]
    share = enc_width // groups
    lanes = 2 * width // 128
    sent = grads.reshape(groups // CORES, CORES, share, lanes, 128).transpose(1, 0, 3, 2, 4)
    sent = sent.reshape(CORES, groups // CORES, lanes * share, 128)
    core = lax.axis_index("dp") % CORES
    mine = lax.dynamic_index_in_dim(sent, core, 0, keepdims=False)
    partner = lax.dynamic_index_in_dim(sent, 1 - core, 0, keepdims=False)
    swap = [(i, i ^ 1) for i in range(groups)]
    both = mine.astype(jnp.float32) + lax.ppermute(partner, "dp", swap).astype(jnp.float32)
    same_core = [list(range(c, groups, CORES)) for c in range(CORES)]
    terms = lax.all_to_all(
        both.astype(jnp.bfloat16),
        "dp",
        split_axis=0,
        concat_axis=0,
        axis_index_groups=same_core,
        tiled=True,
    )
    total = jnp.sum(terms.astype(jnp.float32), axis=0).reshape(lanes, share, 128)
    total = total.transpose(1, 0, 2).reshape(share, 2 * width)
    return attended, total[:, :width], total[:, width:]


def solution(mesh):
    in_specs = (
        P("dp", "head"),
        P("dp", "head", None),
        P("dp", None),
        P("dp", None),
        P(None, "head"),
        P(None, "head"),
        P("dp", "head"),
    )
    out_specs = (P("dp", "head"), P("dp", "head"), P("dp", "head"))
    return jax.shard_map(
        per_device, mesh=mesh, in_specs=in_specs, out_specs=out_specs, check_vma=False
    )
```

```python
import functools

import jax
import jax.numpy as jnp
from jax import lax
from jax.experimental import pallas as pl
from jax.experimental.pallas import tpu as pltpu
from jax.sharding import PartitionSpec as P

HEAD_DIM = 128
STRETCH = 64
MOST = 2
HALVES = 2
CORES = 2
GROUP = 8


def block_diagonal(rows):
    left, right = rows[:, :HEAD_DIM], rows[:, HEAD_DIM:]
    zero = jnp.zeros_like(left)
    return jnp.concatenate(
        [jnp.concatenate([left, zero], axis=1), jnp.concatenate([zero, right], axis=1)], axis=0
    )


def dot_nt(a, b):
    return lax.dot_general(a, b, (((1,), (1,)), ((), ())), preferred_element_type=jnp.float32)


def dot_tn(a, b):
    return lax.dot_general(a, b, (((0,), (0,)), ((), ())), preferred_element_type=jnp.float32)


def attention_kernel(*refs, pieces, rows, last):
    q_ref, g_ref, wk_ref, wv_ref = refs[:4]
    e_refs = refs[4 : 4 + pieces]
    if last:
        sum_ref, _, att_ref, grad_ref, kv_ref, dkv_ref, acc_ref = refs[4 + pieces :]
    else:
        att_ref, acc_ref, kv_ref, dkv_ref = refs[4 + pieces :]
    step = pl.program_id(0)
    width = wk_ref.shape[1]
    score_scale = HEAD_DIM ** (-0.5)
    encoded = jnp.concatenate([e[...] for e in e_refs], axis=0)
    w_both = jnp.concatenate([wk_ref[...], wv_ref[...]], axis=1)
    kv_ref[...] = (
        jnp.dot(encoded, w_both, preferred_element_type=jnp.float32)
        .astype(jnp.bfloat16)
        .reshape(pieces, GROUP * rows, 2 * width)
    )
    keys_total = pieces * rows
    group = range(GROUP)
    tokens = [slice(s * STRETCH, (s + 1) * STRETCH) for s in group]
    q2 = [block_diagonal(q_ref[tokens[s], :]) for s in group]
    g2 = [block_diagonal(g_ref[tokens[s], :]) for s in group]
    kv = [
        kv_ref[:, s * rows : (s + 1) * rows, :].reshape(keys_total, 2 * width) for s in group
    ]
    scores = [dot_nt(kv[s][:, :width], q2[s]) * score_scale for s in group]
    grad_probs = [dot_nt(kv[s][:, width:], g2[s]) for s in group]
    weights = [jnp.exp(x - jnp.max(x, axis=0, keepdims=True)) for x in scores]
    probs = [x * (1.0 / jnp.sum(x, axis=0, keepdims=True)) for x in weights]
    probs_low = [x.astype(jnp.bfloat16) for x in probs]
    inner = [jnp.sum(p * g, axis=0, keepdims=True) for p, g in zip(probs, grad_probs)]
    grad_scores = [
        (p * (g - i)).astype(jnp.bfloat16) for p, g, i in zip(probs, grad_probs, inner)
    ]
    for s in group:
        out2 = dot_tn(probs_low[s], kv[s][:, width:])
        att_ref[tokens[s], :] = jnp.concatenate(
            [out2[:STRETCH, :HEAD_DIM], out2[STRETCH:, HEAD_DIM:]], axis=1
        ).astype(jnp.bfloat16)
        cols = slice(s * keys_total, (s + 1) * keys_total)
        dkv_ref[:width, cols] = (dot_nt(q2[s].T, grad_scores[s]) * score_scale).astype(jnp.bfloat16)
        dkv_ref[width:, cols] = dot_nt(g2[s].T, probs_low[s]).astype(jnp.bfloat16)
    by_stretch = jnp.concatenate(
        [e[s * rows : (s + 1) * rows, :] for s in range(GROUP) for e in e_refs], axis=0
    )
    part = jnp.dot(dkv_ref[...], by_stretch, preferred_element_type=jnp.float32)

    @pl.when(step == 0)
    def _():
        acc_ref[...] = sum_ref[...] + part if last else part

    @pl.when(step > 0)
    def _():
        acc_ref[...] += part

    if last:

        @pl.when(step == pl.num_programs(0) - 1)
        def _():
            grad_ref[...] = acc_ref[...].T.astype(grad_ref.dtype)


def attend(queries, grad_out, w_key, w_value, encoded, half, earlier):
    tokens, width = queries.shape
    enc = w_key.shape[0]
    stretches = tokens // STRETCH // HALVES
    pieces = len(encoded)
    rows = encoded[0].shape[0] // stretches
    keys_total = pieces * rows
    steps = stretches // GROUP
    last = half == HALVES - 1
    token_block = pl.BlockSpec((GROUP * STRETCH, width), lambda i: (half * steps + i, 0))
    whole_w = pl.BlockSpec((enc, width), lambda i: (0, 0))
    sum_block = pl.BlockSpec((2 * width, enc), lambda i: (0, 0))
    sum_shape = jax.ShapeDtypeStruct((2 * width, enc), jnp.float32)
    piece_block = pl.BlockSpec((GROUP * rows, enc), lambda i: (i, 0))
    flops = 2 * stretches * keys_total * enc * 4 * width + 5 * tokens * keys_total * width
    scratch = [
        pltpu.VMEM((pieces, GROUP * rows, 2 * width), jnp.bfloat16),
        pltpu.VMEM((2 * width, GROUP * keys_total), jnp.bfloat16),
    ]
    in_specs = [token_block, token_block, whole_w, whole_w] + [piece_block] * pieces
    att_shape = jax.ShapeDtypeStruct((tokens, width), jnp.bfloat16)
    if last:
        in_specs += [sum_block, pl.BlockSpec(memory_space=pl.ANY)]
        out_specs = [token_block, pl.BlockSpec((enc, 2 * width), lambda i: (0, 0))]
        out_shape = [att_shape, jax.ShapeDtypeStruct((enc, 2 * width), jnp.bfloat16)]
        scratch.append(pltpu.VMEM(sum_shape.shape, sum_shape.dtype))
        aliases = {5 + pieces: 0}
    else:
        out_specs = [token_block, sum_block]
        out_shape = [att_shape, sum_shape]
        aliases = {}
    return pl.pallas_call(
        functools.partial(attention_kernel, pieces=pieces, rows=rows, last=last),
        grid=(steps,),
        in_specs=in_specs,
        out_specs=out_specs,
        out_shape=out_shape,
        scratch_shapes=scratch,
        input_output_aliases=aliases,
        cost_estimate=pl.CostEstimate(
            flops=flops, bytes_accessed=6_000_000, transcendentals=500_000
        ),
        compiler_params=pltpu.CompilerParams(vmem_limit_bytes=40 * 1024 * 1024),
        name="attention",
    )(queries, grad_out, w_key, w_value, *encoded, *earlier)


def pick_kernel(index_ref, source_ref, out_ref, sem):

    @pl.loop(0, out_ref.shape[0])
    def _(i):
        pltpu.make_async_copy(source_ref.at[index_ref[i]], out_ref.at[i], sem).start()

    pltpu.make_async_copy(out_ref, out_ref, sem).wait()


def pick(source, index, source_space, out_space, vmem_limit):
    count = index.shape[0]
    rows, width = source.shape[1:]
    return pl.pallas_call(
        pick_kernel,
        grid_spec=pltpu.PrefetchScalarGridSpec(
            num_scalar_prefetch=1,
            grid=(),
            in_specs=[pl.BlockSpec(memory_space=source_space)],
            out_specs=pl.BlockSpec(memory_space=out_space),
            scratch_shapes=[pltpu.SemaphoreType.DMA],
        ),
        out_shape=jax.ShapeDtypeStruct((count, rows, width), source.dtype),
        cost_estimate=pl.CostEstimate(
            flops=0, bytes_accessed=4 * count * rows * width, transcendentals=0
        ),
        compiler_params=pltpu.CompilerParams(vmem_limit_bytes=vmem_limit),
        name="pick",
    )(index, source)


def slot_ranks(owners):
    slot_count = owners.shape[0]
    row_order = lax.broadcasted_iota(jnp.int32, (slot_count, slot_count), 0)
    col_order = lax.broadcasted_iota(jnp.int32, (slot_count, slot_count), 1)
    same_owner = (owners[:, None] == owners[None, :]) & (row_order < col_order)
    return jnp.sum(same_owner.astype(jnp.int32), axis=0)


def exchange(x):
    return lax.all_to_all(x, "dp", split_axis=0, concat_axis=0, tiled=True)


def ring_gather(x, far_right):
    size = lax.axis_size("head")
    rightward = [(i, (i + 1) % size) for i in range(size)]
    leftward = [(i, (i - 1) % size) for i in range(size)]
    pieces = [x]
    right = left = x
    for _ in range((size - 1) // 2):
        right = lax.ppermute(right, "head", rightward)
        left = lax.ppermute(left, "head", leftward)
        pieces += [right, left]
    if far_right:
        pieces.append(lax.ppermute(right, "head", rightward))
    else:
        pieces.append(lax.ppermute(left, "head", leftward))
    return pieces


def per_device(queries, table, owner, local_id, w_key, w_value, grad_out):
    groups = lax.axis_size("dp")
    owners = owner[:, 0]
    slot_ids = local_id[:, 0]
    slot_count = owners.shape[0]
    slot_rank = slot_ranks(owners)
    pick_index = lax.broadcasted_iota(jnp.int32, (1, 1, MOST), 2)
    owner_index = lax.broadcasted_iota(jnp.int32, (1, groups, 1), 1)
    chosen = (owners[:, None, None] == owner_index) & (slot_rank[:, None, None] == pick_index)
    wanted = jnp.sum(jnp.where(chosen, slot_ids[:, None, None], 0), axis=0)
    asked_ids = exchange(wanted).reshape(-1)
    part, enc_width = table.shape[1:]
    own_index = owners * MOST + slot_rank
    replies = jnp.take(table, asked_ids, axis=0, mode="clip")
    fetched = exchange(replies.reshape(groups, MOST, part, enc_width))
    fetched = fetched.reshape(groups * MOST, part, enc_width)
    half_slots = slot_count // HALVES
    queries, grad_out, w_key, w_value = (
        pltpu.with_memory_space_constraint(x, pltpu.HBM)
        for x in (queries, grad_out, w_key, w_value)
    )
    results = ()
    for half in range(HALVES):
        index = own_index[half * half_slots : (half + 1) * half_slots]
        own = pick(fetched, index, pl.ANY, pl.ANY, 1024 * 1024)
        pieces = ring_gather(own.reshape(half_slots * part, enc_width), half % 2 == 0)
        pieces = [pltpu.with_memory_space_constraint(piece, pltpu.HBM) for piece in pieces]
        results = attend(queries, grad_out, w_key, w_value, pieces, half, results[::-1])
    attended, grads = results
    width = w_key.shape[1]
    share = enc_width // groups
    lanes = 2 * width // 128
    sent = grads.reshape(groups // CORES, CORES, share, lanes, 128).transpose(1, 0, 3, 2, 4)
    sent = sent.reshape(CORES, groups // CORES, lanes * share, 128)
    core = lax.axis_index("dp") % CORES
    mine = lax.dynamic_index_in_dim(sent, core, 0, keepdims=False)
    partner = lax.dynamic_index_in_dim(sent, 1 - core, 0, keepdims=False)
    swap = [(i, i ^ 1) for i in range(groups)]
    both = mine.astype(jnp.float32) + lax.ppermute(partner, "dp", swap).astype(jnp.float32)
    same_core = [list(range(c, groups, CORES)) for c in range(CORES)]
    terms = lax.all_to_all(
        both.astype(jnp.bfloat16),
        "dp",
        split_axis=0,
        concat_axis=0,
        axis_index_groups=same_core,
        tiled=True,
    )
    total = jnp.sum(terms.astype(jnp.float32), axis=0).reshape(lanes, share, 128)
    total = total.transpose(1, 0, 2).reshape(share, 2 * width)
    return attended, total[:, :width], total[:, width:]


def solution(mesh):
    in_specs = (
        P("dp", "head"),
        P("dp", "head", None),
        P("dp", None),
        P("dp", None),
        P(None, "head"),
        P(None, "head"),
        P("dp", "head"),
    )
    out_specs = (P("dp", "head"), P("dp", "head"), P("dp", "head"))
    return jax.shard_map(
        per_device, mesh=mesh, in_specs=in_specs, out_specs=out_specs, check_vma=False
    )
```

```python
import functools

import jax
import jax.numpy as jnp
from jax import lax
from jax.experimental import pallas as pl
from jax.experimental.pallas import tpu as pltpu
from jax.sharding import PartitionSpec as P

HEAD_DIM = 128
STRETCH = 64
MOST = 2
HALVES = 2
CORES = 2
GROUP = 8


def block_diagonal(rows):
    left, right = rows[:, :HEAD_DIM], rows[:, HEAD_DIM:]
    zero = jnp.zeros_like(left)
    return jnp.concatenate(
        [jnp.concatenate([left, zero], axis=1), jnp.concatenate([zero, right], axis=1)], axis=0
    )


def dot_nt(a, b):
    return lax.dot_general(a, b, (((1,), (1,)), ((), ())), preferred_element_type=jnp.float32)


def dot_tn(a, b):
    return lax.dot_general(a, b, (((0,), (0,)), ((), ())), preferred_element_type=jnp.float32)


def attention_kernel(*refs, pieces, rows, last):
    q_ref, g_ref, wk_ref, wv_ref = refs[:4]
    e_refs = refs[4 : 4 + pieces]
    if last:
        sum_ref, _, att_ref, grad_ref, kv_ref, dkv_ref, acc_ref = refs[4 + pieces :]
    else:
        att_ref, acc_ref, kv_ref, dkv_ref = refs[4 + pieces :]
    step = pl.program_id(0)
    width = wk_ref.shape[1]
    score_scale = HEAD_DIM ** (-0.5)
    encoded = jnp.concatenate([e[...] for e in e_refs], axis=0)
    w_both = jnp.concatenate([wk_ref[...], wv_ref[...]], axis=1)
    kv_ref[...] = (
        jnp.dot(encoded, w_both, preferred_element_type=jnp.float32)
        .astype(jnp.bfloat16)
        .reshape(pieces, GROUP * rows, 2 * width)
    )
    keys_total = pieces * rows
    group = range(GROUP)
    tokens = [slice(s * STRETCH, (s + 1) * STRETCH) for s in group]
    q2 = [block_diagonal(q_ref[tokens[s], :]) for s in group]
    g2 = [block_diagonal(g_ref[tokens[s], :]) for s in group]
    kv = [
        kv_ref[:, s * rows : (s + 1) * rows, :].reshape(keys_total, 2 * width) for s in group
    ]
    scores = [dot_nt(kv[s][:, :width], q2[s]) * score_scale for s in group]
    grad_probs = [dot_nt(kv[s][:, width:], g2[s]) for s in group]
    weights = [jnp.exp(x - jnp.max(x, axis=0, keepdims=True)) for x in scores]
    probs = [x * (1.0 / jnp.sum(x, axis=0, keepdims=True)) for x in weights]
    probs_low = [x.astype(jnp.bfloat16) for x in probs]
    inner = [jnp.sum(p * g, axis=0, keepdims=True) for p, g in zip(probs, grad_probs)]
    grad_scores = [
        (p * (g - i)).astype(jnp.bfloat16) for p, g, i in zip(probs, grad_probs, inner)
    ]
    for s in group:
        out2 = dot_tn(probs_low[s], kv[s][:, width:])
        att_ref[tokens[s], :] = jnp.concatenate(
            [out2[:STRETCH, :HEAD_DIM], out2[STRETCH:, HEAD_DIM:]], axis=1
        ).astype(jnp.bfloat16)
        cols = slice(s * keys_total, (s + 1) * keys_total)
        dkv_ref[:width, cols] = (dot_nt(q2[s].T, grad_scores[s]) * score_scale).astype(jnp.bfloat16)
        dkv_ref[width:, cols] = dot_nt(g2[s].T, probs_low[s]).astype(jnp.bfloat16)
    by_stretch = jnp.concatenate(
        [e[s * rows : (s + 1) * rows, :] for s in range(GROUP) for e in e_refs], axis=0
    )
    part = jnp.dot(dkv_ref[...], by_stretch, preferred_element_type=jnp.float32)

    @pl.when(step == 0)
    def _():
        acc_ref[...] = sum_ref[...] + part if last else part

    @pl.when(step > 0)
    def _():
        acc_ref[...] += part

    if last:

        @pl.when(step == pl.num_programs(0) - 1)
        def _():
            grad_ref[...] = acc_ref[...].T.astype(grad_ref.dtype)


def attend(queries, grad_out, w_key, w_value, encoded, half, earlier):
    tokens, width = queries.shape
    enc = w_key.shape[0]
    stretches = tokens // STRETCH // HALVES
    pieces = len(encoded)
    rows = encoded[0].shape[0] // stretches
    keys_total = pieces * rows
    steps = stretches // GROUP
    last = half == HALVES - 1
    token_block = pl.BlockSpec((GROUP * STRETCH, width), lambda i: (half * steps + i, 0))
    whole_w = pl.BlockSpec((enc, width), lambda i: (0, 0))
    sum_block = pl.BlockSpec((2 * width, enc), lambda i: (0, 0))
    sum_shape = jax.ShapeDtypeStruct((2 * width, enc), jnp.float32)
    piece_block = pl.BlockSpec((GROUP * rows, enc), lambda i: (i, 0))
    flops = 2 * stretches * keys_total * enc * 4 * width + 5 * tokens * keys_total * width
    scratch = [
        pltpu.VMEM((pieces, GROUP * rows, 2 * width), jnp.bfloat16),
        pltpu.VMEM((2 * width, GROUP * keys_total), jnp.bfloat16),
    ]
    in_specs = [token_block, token_block, whole_w, whole_w] + [piece_block] * pieces
    att_shape = jax.ShapeDtypeStruct((tokens, width), jnp.bfloat16)
    if last:
        in_specs += [sum_block, pl.BlockSpec(memory_space=pl.ANY)]
        out_specs = [token_block, pl.BlockSpec((enc, 2 * width), lambda i: (0, 0))]
        out_shape = [att_shape, jax.ShapeDtypeStruct((enc, 2 * width), jnp.bfloat16)]
        scratch.append(pltpu.VMEM(sum_shape.shape, sum_shape.dtype))
        aliases = {5 + pieces: 0}
    else:
        out_specs = [token_block, sum_block]
        out_shape = [att_shape, sum_shape]
        aliases = {}
    return pl.pallas_call(
        functools.partial(attention_kernel, pieces=pieces, rows=rows, last=last),
        grid=(steps,),
        in_specs=in_specs,
        out_specs=out_specs,
        out_shape=out_shape,
        scratch_shapes=scratch,
        input_output_aliases=aliases,
        cost_estimate=pl.CostEstimate(
            flops=flops, bytes_accessed=6_000_000, transcendentals=500_000
        ),
        compiler_params=pltpu.CompilerParams(vmem_limit_bytes=40 * 1024 * 1024),
        name="attention",
    )(queries, grad_out, w_key, w_value, *encoded, *earlier)


def pick_kernel(index_ref, source_ref, out_ref, sem):

    @pl.loop(0, out_ref.shape[0])
    def _(i):
        pltpu.make_async_copy(source_ref.at[index_ref[i]], out_ref.at[i], sem).start()

    pltpu.make_async_copy(out_ref, out_ref, sem).wait()


def pick(source, index, source_space, out_space, vmem_limit):
    count = index.shape[0]
    rows, width = source.shape[1:]
    return pl.pallas_call(
        pick_kernel,
        grid_spec=pltpu.PrefetchScalarGridSpec(
            num_scalar_prefetch=1,
            grid=(),
            in_specs=[pl.BlockSpec(memory_space=source_space)],
            out_specs=pl.BlockSpec(memory_space=out_space),
            scratch_shapes=[pltpu.SemaphoreType.DMA],
        ),
        out_shape=jax.ShapeDtypeStruct((count, rows, width), source.dtype),
        cost_estimate=pl.CostEstimate(
            flops=0, bytes_accessed=4 * count * rows * width, transcendentals=0
        ),
        compiler_params=pltpu.CompilerParams(vmem_limit_bytes=vmem_limit),
        name="pick",
    )(index, source)


def slot_ranks(owners):
    slot_count = owners.shape[0]
    row_order = lax.broadcasted_iota(jnp.int32, (slot_count, slot_count), 0)
    col_order = lax.broadcasted_iota(jnp.int32, (slot_count, slot_count), 1)
    same_owner = (owners[:, None] == owners[None, :]) & (row_order < col_order)
    return jnp.sum(same_owner.astype(jnp.int32), axis=0)


def exchange(x):
    return lax.all_to_all(x, "dp", split_axis=0, concat_axis=0, tiled=True)


def ring_gather(halves):
    size = lax.axis_size("head")
    rightward = [(i, (i + 1) % size) for i in range(size)]
    leftward = [(i, (i - 1) % size) for i in range(size)]
    pieces = [[x] for x in halves]
    right, left = list(halves), list(halves)
    rounds = (size - 1) // 2
    for turn in range(rounds):
        for half in range(HALVES):
            if turn == rounds - 1 and half == 1:
                gated = lax.optimization_barrier((right[0], left[0], right[1], left[1]))
                right[0], left[0], right[1], left[1] = gated
                pieces[0][-2:] = gated[:2]
                pieces[1][-2:] = gated[2:]
                pieces[0].append(lax.ppermute(right[0], "head", rightward))
            right[half] = lax.ppermute(right[half], "head", rightward)
            left[half] = lax.ppermute(left[half], "head", leftward)
            pieces[half] += [right[half], left[half]]
    pieces[1].append(lax.ppermute(left[1], "head", leftward))
    return pieces


def per_device(queries, table, owner, local_id, w_key, w_value, grad_out):
    groups = lax.axis_size("dp")
    owners = owner[:, 0]
    slot_ids = local_id[:, 0]
    slot_count = owners.shape[0]
    slot_rank = slot_ranks(owners)
    pick_index = lax.broadcasted_iota(jnp.int32, (1, 1, MOST), 2)
    owner_index = lax.broadcasted_iota(jnp.int32, (1, groups, 1), 1)
    chosen = (owners[:, None, None] == owner_index) & (slot_rank[:, None, None] == pick_index)
    wanted = jnp.sum(jnp.where(chosen, slot_ids[:, None, None], 0), axis=0)
    asked_ids = exchange(wanted).reshape(-1)
    part, enc_width = table.shape[1:]
    own_index = owners * MOST + slot_rank
    replies = jnp.take(table, asked_ids, axis=0, mode="clip")
    fetched = exchange(replies.reshape(groups, MOST, part, enc_width))
    fetched = fetched.reshape(groups * MOST, part, enc_width)
    half_slots = slot_count // HALVES
    queries, grad_out, w_key, w_value = (
        pltpu.with_memory_space_constraint(x, pltpu.HBM)
        for x in (queries, grad_out, w_key, w_value)
    )
    own = []
    for half in range(HALVES):
        index = own_index[half * half_slots : (half + 1) * half_slots]
        rows = pick(fetched, index, pl.ANY, pl.ANY, 1024 * 1024)
        own.append(rows.reshape(half_slots * part, enc_width))
    results = ()
    for half, pieces in enumerate(ring_gather(own)):
        pieces = [pltpu.with_memory_space_constraint(piece, pltpu.HBM) for piece in pieces]
        results = attend(queries, grad_out, w_key, w_value, pieces, half, results[::-1])
    attended, grads = results
    width = w_key.shape[1]
    share = enc_width // groups
    lanes = 2 * width // 128
    sent = grads.reshape(groups // CORES, CORES, share, lanes, 128).transpose(1, 0, 3, 2, 4)
    sent = sent.reshape(CORES, groups // CORES, lanes * share, 128)
    core = lax.axis_index("dp") % CORES
    mine = lax.dynamic_index_in_dim(sent, core, 0, keepdims=False)
    partner = lax.dynamic_index_in_dim(sent, 1 - core, 0, keepdims=False)
    swap = [(i, i ^ 1) for i in range(groups)]
    both = mine.astype(jnp.float32) + lax.ppermute(partner, "dp", swap).astype(jnp.float32)
    same_core = [list(range(c, groups, CORES)) for c in range(CORES)]
    terms = lax.all_to_all(
        both.astype(jnp.bfloat16),
        "dp",
        split_axis=0,
        concat_axis=0,
        axis_index_groups=same_core,
        tiled=True,
    )
    total = jnp.sum(terms.astype(jnp.float32), axis=0).reshape(lanes, share, 128)
    total = total.transpose(1, 0, 2).reshape(share, 2 * width)
    return attended, total[:, :width], total[:, width:]


def solution(mesh):
    in_specs = (
        P("dp", "head"),
        P("dp", "head", None),
        P("dp", None),
        P("dp", None),
        P(None, "head"),
        P(None, "head"),
        P("dp", "head"),
    )
    out_specs = (P("dp", "head"), P("dp", "head"), P("dp", "head"))
    return jax.shard_map(
        per_device, mesh=mesh, in_specs=in_specs, out_specs=out_specs, check_vma=False
    )
```

```python
import functools

import jax
import jax.numpy as jnp
from jax import lax
from jax.experimental import pallas as pl
from jax.experimental.pallas import tpu as pltpu
from jax.sharding import PartitionSpec as P

HEAD_DIM = 128
STRETCH = 64
MOST = 2
HALVES = 2
CORES = 2
GROUP = 8


def block_diagonal(rows):
    left, right = rows[:, :HEAD_DIM], rows[:, HEAD_DIM:]
    zero = jnp.zeros_like(left)
    return jnp.concatenate(
        [jnp.concatenate([left, zero], axis=1), jnp.concatenate([zero, right], axis=1)], axis=0
    )


def dot_nt(a, b):
    return lax.dot_general(a, b, (((1,), (1,)), ((), ())), preferred_element_type=jnp.float32)


def dot_tn(a, b):
    return lax.dot_general(a, b, (((0,), (0,)), ((), ())), preferred_element_type=jnp.float32)


def attention_kernel(*refs, pieces, rows, last):
    q_ref, g_ref, wk_ref, wv_ref = refs[:4]
    e_refs = refs[4 : 4 + pieces]
    if last:
        sum_ref, _, att_ref, grad_ref, kv_ref, dkv_ref, acc_ref = refs[4 + pieces :]
    else:
        att_ref, acc_ref, kv_ref, dkv_ref = refs[4 + pieces :]
    step = pl.program_id(0)
    width = wk_ref.shape[1]
    score_scale = HEAD_DIM ** (-0.5)
    encoded = jnp.concatenate([e[...] for e in e_refs], axis=0)
    w_both = jnp.concatenate([wk_ref[...], wv_ref[...]], axis=1)
    kv_ref[...] = (
        jnp.dot(encoded, w_both, preferred_element_type=jnp.float32)
        .astype(jnp.bfloat16)
        .reshape(pieces, GROUP * rows, 2 * width)
    )
    keys_total = pieces * rows
    group = range(GROUP)
    tokens = [slice(s * STRETCH, (s + 1) * STRETCH) for s in group]
    q2 = [block_diagonal(q_ref[tokens[s], :]) for s in group]
    g2 = [block_diagonal(g_ref[tokens[s], :]) for s in group]
    kv = [
        kv_ref[:, s * rows : (s + 1) * rows, :].reshape(keys_total, 2 * width) for s in group
    ]
    scores = [dot_nt(kv[s][:, :width], q2[s]) * score_scale for s in group]
    grad_probs = [dot_nt(kv[s][:, width:], g2[s]) for s in group]
    weights = [jnp.exp(x - jnp.max(x, axis=0, keepdims=True)) for x in scores]
    probs = [x * (1.0 / jnp.sum(x, axis=0, keepdims=True)) for x in weights]
    probs_low = [x.astype(jnp.bfloat16) for x in probs]
    inner = [jnp.sum(p * g, axis=0, keepdims=True) for p, g in zip(probs, grad_probs)]
    grad_scores = [
        (p * (g - i)).astype(jnp.bfloat16) for p, g, i in zip(probs, grad_probs, inner)
    ]
    for s in group:
        out2 = dot_tn(probs_low[s], kv[s][:, width:])
        att_ref[tokens[s], :] = jnp.concatenate(
            [out2[:STRETCH, :HEAD_DIM], out2[STRETCH:, HEAD_DIM:]], axis=1
        ).astype(jnp.bfloat16)
        cols = slice(s * keys_total, (s + 1) * keys_total)
        dkv_ref[:width, cols] = (dot_nt(q2[s].T, grad_scores[s]) * score_scale).astype(jnp.bfloat16)
        dkv_ref[width:, cols] = dot_nt(g2[s].T, probs_low[s]).astype(jnp.bfloat16)
    by_stretch = jnp.concatenate(
        [e[s * rows : (s + 1) * rows, :] for s in range(GROUP) for e in e_refs], axis=0
    )
    part = jnp.dot(dkv_ref[...], by_stretch, preferred_element_type=jnp.float32)

    @pl.when(step == 0)
    def _():
        acc_ref[...] = sum_ref[...] + part if last else part

    @pl.when(step > 0)
    def _():
        acc_ref[...] += part

    if last:

        @pl.when(step == pl.num_programs(0) - 1)
        def _():
            grad_ref[...] = acc_ref[...].T.astype(grad_ref.dtype)


def attend(queries, grad_out, w_key, w_value, encoded, half, earlier):
    tokens, width = queries.shape
    enc = w_key.shape[0]
    stretches = tokens // STRETCH // HALVES
    pieces = len(encoded)
    rows = encoded[0].shape[0] // stretches
    keys_total = pieces * rows
    steps = stretches // GROUP
    last = half == HALVES - 1
    token_block = pl.BlockSpec((GROUP * STRETCH, width), lambda i: (half * steps + i, 0))
    whole_w = pl.BlockSpec((enc, width), lambda i: (0, 0))
    sum_block = pl.BlockSpec((2 * width, enc), lambda i: (0, 0))
    sum_shape = jax.ShapeDtypeStruct((2 * width, enc), jnp.float32)
    piece_block = pl.BlockSpec((GROUP * rows, enc), lambda i: (i, 0))
    flops = 2 * stretches * keys_total * enc * 4 * width + 5 * tokens * keys_total * width
    scratch = [
        pltpu.VMEM((pieces, GROUP * rows, 2 * width), jnp.bfloat16),
        pltpu.VMEM((2 * width, GROUP * keys_total), jnp.bfloat16),
    ]
    in_specs = [token_block, token_block, whole_w, whole_w] + [piece_block] * pieces
    att_shape = jax.ShapeDtypeStruct((tokens, width), jnp.bfloat16)
    if last:
        in_specs += [sum_block, pl.BlockSpec(memory_space=pl.ANY)]
        out_specs = [token_block, pl.BlockSpec((enc, 2 * width), lambda i: (0, 0))]
        out_shape = [att_shape, jax.ShapeDtypeStruct((enc, 2 * width), jnp.bfloat16)]
        scratch.append(pltpu.VMEM(sum_shape.shape, sum_shape.dtype))
        aliases = {5 + pieces: 0}
    else:
        out_specs = [token_block, sum_block]
        out_shape = [att_shape, sum_shape]
        aliases = {}
    return pl.pallas_call(
        functools.partial(attention_kernel, pieces=pieces, rows=rows, last=last),
        grid=(steps,),
        in_specs=in_specs,
        out_specs=out_specs,
        out_shape=out_shape,
        scratch_shapes=scratch,
        input_output_aliases=aliases,
        cost_estimate=pl.CostEstimate(
            flops=flops, bytes_accessed=6_000_000, transcendentals=500_000
        ),
        compiler_params=pltpu.CompilerParams(vmem_limit_bytes=40 * 1024 * 1024),
        name="attention",
    )(queries, grad_out, w_key, w_value, *encoded, *earlier)


def pick_kernel(index_ref, source_ref, *refs):
    *outs, sem = refs
    for half, out_ref in enumerate(outs):
        count = out_ref.shape[0]

        @pl.loop(0, count)
        def _(i):
            row = source_ref.at[index_ref[half * count + i]]
            pltpu.make_async_copy(row, out_ref.at[i], sem.at[half]).start()

    for half, out_ref in enumerate(outs):
        pltpu.make_async_copy(out_ref, out_ref, sem.at[half]).wait()


def pick(source, index):
    count = index.shape[0] // HALVES
    rows, width = source.shape[1:]
    return pl.pallas_call(
        pick_kernel,
        grid_spec=pltpu.PrefetchScalarGridSpec(
            num_scalar_prefetch=1,
            grid=(),
            in_specs=[pl.BlockSpec(memory_space=pl.ANY)],
            out_specs=[pl.BlockSpec(memory_space=pl.ANY)] * HALVES,
            scratch_shapes=[pltpu.SemaphoreType.DMA((HALVES,))],
        ),
        out_shape=[jax.ShapeDtypeStruct((count, rows, width), source.dtype)] * HALVES,
        cost_estimate=pl.CostEstimate(
            flops=0, bytes_accessed=8 * count * rows * width, transcendentals=0
        ),
        compiler_params=pltpu.CompilerParams(vmem_limit_bytes=1024 * 1024),
        name="pick",
    )(index, source)


def request_kernel(owner_ref, id_ref, wanted_ref, own_ref):
    groups, lanes = wanted_ref.shape
    slots = owner_ref.shape[1]
    owners = owner_ref[...]
    ids = id_ref[...].astype(jnp.float32)
    match = lax.broadcasted_iota(jnp.int32, (groups, slots), 0) == owners
    row = lax.broadcasted_iota(jnp.int32, (slots, slots), 0)
    col = lax.broadcasted_iota(jnp.int32, (slots, slots), 1)
    rank = jnp.dot(
        match.astype(jnp.bfloat16),
        (row < col).astype(jnp.bfloat16),
        preferred_element_type=jnp.float32,
    )
    lane = lax.broadcasted_iota(jnp.int32, (groups, lanes), 1)
    wanted = jnp.zeros((groups, lanes), jnp.float32)
    for turn in range(MOST):
        asked = jnp.where(match & (rank == turn), ids, 0.0)
        wanted = jnp.where(lane == turn, jnp.sum(asked, axis=1, keepdims=True), wanted)
    wanted_ref[...] = wanted.astype(jnp.int32)
    own_rank = jnp.sum(jnp.where(match, rank, 0.0), axis=0, keepdims=True)
    own_ref[...] = owners * MOST + own_rank.astype(jnp.int32)


def requests(owner, local_id, groups):
    slots = owner.shape[0]
    return pl.pallas_call(
        request_kernel,
        out_shape=[
            jax.ShapeDtypeStruct((groups, 128), jnp.int32),
            jax.ShapeDtypeStruct((1, slots), jnp.int32),
        ],
        name="requests",
    )(owner.reshape(1, slots), local_id.reshape(1, slots))


def exchange(x):
    return lax.all_to_all(x, "dp", split_axis=0, concat_axis=0, tiled=True)


def ring_gather(x, far_right):
    size = lax.axis_size("head")
    rightward = [(i, (i + 1) % size) for i in range(size)]
    leftward = [(i, (i - 1) % size) for i in range(size)]
    pieces = [x]
    right = left = x
    for _ in range((size - 1) // 2):
        right = lax.ppermute(right, "head", rightward)
        left = lax.ppermute(left, "head", leftward)
        pieces += [right, left]
    if far_right:
        pieces.append(lax.ppermute(right, "head", rightward))
    else:
        pieces.append(lax.ppermute(left, "head", leftward))
    return pieces


def per_device(queries, table, owner, local_id, w_key, w_value, grad_out):
    groups = lax.axis_size("dp")
    slot_count = owner.shape[0]
    wanted, own_index = requests(owner, local_id, groups)
    asked_ids = exchange(wanted)[:, :MOST].reshape(-1)
    own_index = own_index.reshape(slot_count)
    part, enc_width = table.shape[1:]
    replies = jnp.take(table, asked_ids, axis=0, mode="clip")
    fetched = exchange(replies.reshape(groups, MOST, part, enc_width))
    fetched = fetched.reshape(groups * MOST, part, enc_width)
    queries, grad_out, w_key, w_value = (
        pltpu.with_memory_space_constraint(x, pltpu.HBM)
        for x in (queries, grad_out, w_key, w_value)
    )
    own = pick(fetched, own_index)
    results = ()
    for half in range(HALVES):
        pieces = ring_gather(own[half].reshape(-1, enc_width), half % 2 == 0)
        pieces = [pltpu.with_memory_space_constraint(piece, pltpu.HBM) for piece in pieces]
        results = attend(queries, grad_out, w_key, w_value, pieces, half, results[::-1])
    attended, grads = results
    width = w_key.shape[1]
    share = enc_width // groups
    lanes = 2 * width // 128
    sent = grads.reshape(groups // CORES, CORES, share, lanes, 128).transpose(1, 0, 3, 2, 4)
    sent = sent.reshape(CORES, groups // CORES, lanes * share, 128)
    core = lax.axis_index("dp") % CORES
    mine = lax.dynamic_index_in_dim(sent, core, 0, keepdims=False)
    partner = lax.dynamic_index_in_dim(sent, 1 - core, 0, keepdims=False)
    swap = [(i, i ^ 1) for i in range(groups)]
    both = mine.astype(jnp.float32) + lax.ppermute(partner, "dp", swap).astype(jnp.float32)
    same_core = [list(range(c, groups, CORES)) for c in range(CORES)]
    terms = lax.all_to_all(
        both.astype(jnp.bfloat16),
        "dp",
        split_axis=0,
        concat_axis=0,
        axis_index_groups=same_core,
        tiled=True,
    )
    total = jnp.sum(terms.astype(jnp.float32), axis=0).reshape(lanes, share, 128)
    total = total.transpose(1, 0, 2).reshape(share, 2 * width)
    return attended, total[:, :width], total[:, width:]


def solution(mesh):
    in_specs = (
        P("dp", "head"),
        P("dp", "head", None),
        P("dp", None),
        P("dp", None),
        P(None, "head"),
        P(None, "head"),
        P("dp", "head"),
    )
    out_specs = (P("dp", "head"), P("dp", "head"), P("dp", "head"))
    return jax.shard_map(
        per_device, mesh=mesh, in_specs=in_specs, out_specs=out_specs, check_vma=False
    )
```

```python
import functools

import jax
import jax.numpy as jnp
from jax import lax
from jax.experimental import pallas as pl
from jax.experimental.pallas import tpu as pltpu
from jax.sharding import PartitionSpec as P

HEAD_DIM = 128
STRETCH = 64
MOST = 2
HALVES = 2
CORES = 2
GROUP = 8
EARLY = 5


def block_diagonal(rows):
    left, right = rows[:, :HEAD_DIM], rows[:, HEAD_DIM:]
    zero = jnp.zeros_like(left)
    return jnp.concatenate(
        [jnp.concatenate([left, zero], axis=1), jnp.concatenate([zero, right], axis=1)], axis=0
    )


def dot_nt(a, b):
    return lax.dot_general(a, b, (((1,), (1,)), ((), ())), preferred_element_type=jnp.float32)


def dot_tn(a, b):
    return lax.dot_general(a, b, (((0,), (0,)), ((), ())), preferred_element_type=jnp.float32)


def attention_kernel(*refs, pieces, rows, last):
    q_ref, g_ref, wk_ref, wv_ref = refs[:4]
    e_refs = refs[4 : 4 + pieces]
    early_refs = refs[4 + pieces : 4 + pieces + EARLY]
    if last:
        sum_ref, _, att_ref, grad_ref, kv_ref, dkv_ref, acc_ref = refs[4 + pieces + EARLY :]
    else:
        att_ref, acc_ref, kv_ref, dkv_ref = refs[4 + pieces + EARLY :]
    step = pl.program_id(0)
    width = wk_ref.shape[1]
    score_scale = HEAD_DIM ** (-0.5)
    encoded = jnp.concatenate([e[...] for e in e_refs[EARLY:]], axis=0)
    w_both = jnp.concatenate([wk_ref[...], wv_ref[...]], axis=1)
    kv_ref[...] = (
        jnp.dot(encoded, w_both, preferred_element_type=jnp.float32)
        .astype(jnp.bfloat16)
        .reshape(pieces - EARLY, GROUP * rows, 2 * width)
    )
    keys_total = pieces * rows
    group = range(GROUP)
    tokens = [slice(s * STRETCH, (s + 1) * STRETCH) for s in group]
    q2 = [block_diagonal(q_ref[tokens[s], :]) for s in group]
    g2 = [block_diagonal(g_ref[tokens[s], :]) for s in group]
    kv = [
        jnp.concatenate(
            [k[s * rows : (s + 1) * rows, :] for k in early_refs]
            + [kv_ref[p, s * rows : (s + 1) * rows, :] for p in range(pieces - EARLY)],
            axis=0,
        )
        for s in group
    ]
    scores = [dot_nt(kv[s][:, :width], q2[s]) * score_scale for s in group]
    grad_probs = [dot_nt(kv[s][:, width:], g2[s]) for s in group]
    weights = [jnp.exp(x - jnp.max(x, axis=0, keepdims=True)) for x in scores]
    probs = [x * (1.0 / jnp.sum(x, axis=0, keepdims=True)) for x in weights]
    probs_low = [x.astype(jnp.bfloat16) for x in probs]
    inner = [jnp.sum(p * g, axis=0, keepdims=True) for p, g in zip(probs, grad_probs)]
    grad_scores = [
        (p * (g - i)).astype(jnp.bfloat16) for p, g, i in zip(probs, grad_probs, inner)
    ]
    for s in group:
        out2 = dot_tn(probs_low[s], kv[s][:, width:])
        att_ref[tokens[s], :] = jnp.concatenate(
            [out2[:STRETCH, :HEAD_DIM], out2[STRETCH:, HEAD_DIM:]], axis=1
        ).astype(jnp.bfloat16)
        cols = slice(s * keys_total, (s + 1) * keys_total)
        dkv_ref[:width, cols] = (dot_nt(q2[s].T, grad_scores[s]) * score_scale).astype(jnp.bfloat16)
        dkv_ref[width:, cols] = dot_nt(g2[s].T, probs_low[s]).astype(jnp.bfloat16)
    by_stretch = jnp.concatenate(
        [e[s * rows : (s + 1) * rows, :] for s in range(GROUP) for e in e_refs], axis=0
    )
    part = jnp.dot(dkv_ref[...], by_stretch, preferred_element_type=jnp.float32)

    @pl.when(step == 0)
    def _():
        acc_ref[...] = sum_ref[...] + part if last else part

    @pl.when(step > 0)
    def _():
        acc_ref[...] += part

    if last:

        @pl.when(step == pl.num_programs(0) - 1)
        def _():
            grad_ref[...] = acc_ref[...].T.astype(grad_ref.dtype)


def attend(queries, grad_out, w_key, w_value, encoded, early, half, earlier):
    tokens, width = queries.shape
    enc = w_key.shape[0]
    stretches = tokens // STRETCH // HALVES
    pieces = len(encoded)
    rows = encoded[0].shape[0] // stretches
    keys_total = pieces * rows
    steps = stretches // GROUP
    last = half == HALVES - 1
    token_block = pl.BlockSpec((GROUP * STRETCH, width), lambda i: (half * steps + i, 0))
    whole_w = pl.BlockSpec((enc, width), lambda i: (0, 0))
    sum_block = pl.BlockSpec((2 * width, enc), lambda i: (0, 0))
    sum_shape = jax.ShapeDtypeStruct((2 * width, enc), jnp.float32)
    piece_block = pl.BlockSpec((GROUP * rows, enc), lambda i: (i, 0))
    flops = 2 * stretches * keys_total * enc * 4 * width + 5 * tokens * keys_total * width
    scratch = [
        pltpu.VMEM((pieces - EARLY, GROUP * rows, 2 * width), jnp.bfloat16),
        pltpu.VMEM((2 * width, GROUP * keys_total), jnp.bfloat16),
    ]
    in_specs = [token_block, token_block, whole_w, whole_w] + [piece_block] * pieces
    in_specs += [pl.BlockSpec((GROUP * rows, 2 * width), lambda i: (i, 0))] * EARLY
    att_shape = jax.ShapeDtypeStruct((tokens, width), jnp.bfloat16)
    if last:
        in_specs += [sum_block, pl.BlockSpec(memory_space=pl.ANY)]
        out_specs = [token_block, pl.BlockSpec((enc, 2 * width), lambda i: (0, 0))]
        out_shape = [att_shape, jax.ShapeDtypeStruct((enc, 2 * width), jnp.bfloat16)]
        scratch.append(pltpu.VMEM(sum_shape.shape, sum_shape.dtype))
        aliases = {5 + pieces + EARLY: 0}
    else:
        out_specs = [token_block, sum_block]
        out_shape = [att_shape, sum_shape]
        aliases = {}
    return pl.pallas_call(
        functools.partial(attention_kernel, pieces=pieces, rows=rows, last=last),
        grid=(steps,),
        in_specs=in_specs,
        out_specs=out_specs,
        out_shape=out_shape,
        scratch_shapes=scratch,
        input_output_aliases=aliases,
        cost_estimate=pl.CostEstimate(
            flops=flops, bytes_accessed=6_000_000, transcendentals=500_000
        ),
        compiler_params=pltpu.CompilerParams(vmem_limit_bytes=40 * 1024 * 1024),
        name="attention",
    )(queries, grad_out, w_key, w_value, *encoded, *early, *earlier)


def pick_kernel(index_ref, source_ref, *refs):
    *outs, sem = refs
    for half, out_ref in enumerate(outs):
        count = out_ref.shape[0]

        @pl.loop(0, count)
        def _(i):
            row = source_ref.at[index_ref[half * count + i]]
            pltpu.make_async_copy(row, out_ref.at[i], sem.at[half]).start()

    for half, out_ref in enumerate(outs):
        pltpu.make_async_copy(out_ref, out_ref, sem.at[half]).wait()


def pick(source, index):
    count = index.shape[0] // HALVES
    rows, width = source.shape[1:]
    return pl.pallas_call(
        pick_kernel,
        grid_spec=pltpu.PrefetchScalarGridSpec(
            num_scalar_prefetch=1,
            grid=(),
            in_specs=[pl.BlockSpec(memory_space=pl.ANY)],
            out_specs=[pl.BlockSpec(memory_space=pl.ANY)] * HALVES,
            scratch_shapes=[pltpu.SemaphoreType.DMA((HALVES,))],
        ),
        out_shape=[jax.ShapeDtypeStruct((count, rows, width), source.dtype)] * HALVES,
        cost_estimate=pl.CostEstimate(
            flops=0, bytes_accessed=8 * count * rows * width, transcendentals=0
        ),
        compiler_params=pltpu.CompilerParams(vmem_limit_bytes=1024 * 1024),
        name="pick",
    )(index, source)


def request_kernel(owner_ref, id_ref, wanted_ref, own_ref):
    groups, lanes = wanted_ref.shape
    slots = owner_ref.shape[1]
    owners = owner_ref[...]
    ids = id_ref[...].astype(jnp.float32)
    match = lax.broadcasted_iota(jnp.int32, (groups, slots), 0) == owners
    row = lax.broadcasted_iota(jnp.int32, (slots, slots), 0)
    col = lax.broadcasted_iota(jnp.int32, (slots, slots), 1)
    rank = jnp.dot(
        match.astype(jnp.bfloat16),
        (row < col).astype(jnp.bfloat16),
        preferred_element_type=jnp.float32,
    )
    lane = lax.broadcasted_iota(jnp.int32, (groups, lanes), 1)
    wanted = jnp.zeros((groups, lanes), jnp.float32)
    for turn in range(MOST):
        asked = jnp.where(match & (rank == turn), ids, 0.0)
        wanted = jnp.where(lane == turn, jnp.sum(asked, axis=1, keepdims=True), wanted)
    wanted_ref[...] = wanted.astype(jnp.int32)
    own_rank = jnp.sum(jnp.where(match, rank, 0.0), axis=0, keepdims=True)
    own_ref[...] = owners * MOST + own_rank.astype(jnp.int32)


def requests(owner, local_id, groups):
    slots = owner.shape[0]
    return pl.pallas_call(
        request_kernel,
        out_shape=[
            jax.ShapeDtypeStruct((groups, 128), jnp.int32),
            jax.ShapeDtypeStruct((1, slots), jnp.int32),
        ],
        name="requests",
    )(owner.reshape(1, slots), local_id.reshape(1, slots))


def exchange(x):
    return lax.all_to_all(x, "dp", split_axis=0, concat_axis=0, tiled=True)


def ring_gather(x, far_right):
    size = lax.axis_size("head")
    rightward = [(i, (i + 1) % size) for i in range(size)]
    leftward = [(i, (i - 1) % size) for i in range(size)]
    pieces = [x]
    right = left = x
    for _ in range((size - 1) // 2):
        right = lax.ppermute(right, "head", rightward)
        left = lax.ppermute(left, "head", leftward)
        pieces += [right, left]
    if far_right:
        pieces.append(lax.ppermute(right, "head", rightward))
    else:
        pieces.append(lax.ppermute(left, "head", leftward))
    return pieces


def per_device(queries, table, owner, local_id, w_key, w_value, grad_out):
    groups = lax.axis_size("dp")
    slot_count = owner.shape[0]
    wanted, own_index = requests(owner, local_id, groups)
    asked_ids = exchange(wanted)[:, :MOST].reshape(-1)
    own_index = own_index.reshape(slot_count)
    part, enc_width = table.shape[1:]
    replies = jnp.take(table, asked_ids, axis=0, mode="clip")
    fetched = exchange(replies.reshape(groups, MOST, part, enc_width))
    fetched = fetched.reshape(groups * MOST, part, enc_width)
    w_both = jnp.concatenate([w_key, w_value], axis=1)
    queries, grad_out, w_key, w_value = (
        pltpu.with_memory_space_constraint(x, pltpu.HBM)
        for x in (queries, grad_out, w_key, w_value)
    )
    own = pick(fetched, own_index)
    results = ()
    for half in range(HALVES):
        pieces = ring_gather(own[half].reshape(-1, enc_width), half % 2 == 0)
        early = [
            jnp.dot(piece, w_both, preferred_element_type=jnp.float32).astype(jnp.bfloat16)
            for piece in pieces[:EARLY]
        ]
        pieces[:EARLY] = [
            pltpu.with_memory_space_constraint(piece, pltpu.HBM) for piece in pieces[:EARLY]
        ]
        early = [pltpu.with_memory_space_constraint(piece, pltpu.HBM) for piece in early]
        results = attend(
            queries, grad_out, w_key, w_value, pieces, early, half, results[::-1]
        )
    attended, grads = results
    width = w_key.shape[1]
    share = enc_width // groups
    lanes = 2 * width // 128
    sent = grads.reshape(groups // CORES, CORES, share, lanes, 128).transpose(1, 0, 3, 2, 4)
    sent = sent.reshape(CORES, groups // CORES, lanes * share, 128)
    core = lax.axis_index("dp") % CORES
    mine = lax.dynamic_index_in_dim(sent, core, 0, keepdims=False)
    partner = lax.dynamic_index_in_dim(sent, 1 - core, 0, keepdims=False)
    swap = [(i, i ^ 1) for i in range(groups)]
    both = mine.astype(jnp.float32) + lax.ppermute(partner, "dp", swap).astype(jnp.float32)
    same_core = [list(range(c, groups, CORES)) for c in range(CORES)]
    terms = lax.all_to_all(
        both.astype(jnp.bfloat16),
        "dp",
        split_axis=0,
        concat_axis=0,
        axis_index_groups=same_core,
        tiled=True,
    )
    total = jnp.sum(terms.astype(jnp.float32), axis=0).reshape(lanes, share, 128)
    total = total.transpose(1, 0, 2).reshape(share, 2 * width)
    return attended, total[:, :width], total[:, width:]


def solution(mesh):
    in_specs = (
        P("dp", "head"),
        P("dp", "head", None),
        P("dp", None),
        P("dp", None),
        P(None, "head"),
        P(None, "head"),
        P("dp", "head"),
    )
    out_specs = (P("dp", "head"), P("dp", "head"), P("dp", "head"))
    return jax.shard_map(
        per_device, mesh=mesh, in_specs=in_specs, out_specs=out_specs, check_vma=False
    )
```

```python
import functools

import jax
import jax.numpy as jnp
from jax import lax
from jax.experimental import pallas as pl
from jax.experimental.pallas import tpu as pltpu
from jax.sharding import PartitionSpec as P

HEAD_DIM = 128
STRETCH = 64
MOST = 2
HALVES = 2
CORES = 2
GROUP = 8
EARLY = 5


def block_diagonal(rows):
    left, right = rows[:, :HEAD_DIM], rows[:, HEAD_DIM:]
    zero = jnp.zeros_like(left)
    return jnp.concatenate(
        [jnp.concatenate([left, zero], axis=1), jnp.concatenate([zero, right], axis=1)], axis=0
    )


def dot_nt(a, b):
    return lax.dot_general(a, b, (((1,), (1,)), ((), ())), preferred_element_type=jnp.float32)


def dot_tn(a, b):
    return lax.dot_general(a, b, (((0,), (0,)), ((), ())), preferred_element_type=jnp.float32)


def attention_kernel(*refs, pieces, rows, last):
    q_ref, g_ref, wk_ref, wv_ref = refs[:4]
    e_refs = refs[4 : 4 + pieces]
    if last:
        sum_ref, _, att_ref, grad_ref, kv_ref, dkv_ref, acc_ref = refs[4 + pieces :]
    else:
        att_ref, acc_ref, kv_ref, dkv_ref = refs[4 + pieces :]
    step = pl.program_id(0)
    width = wk_ref.shape[1]
    score_scale = HEAD_DIM ** (-0.5)
    encoded = jnp.concatenate([e[...] for e in e_refs], axis=0)
    w_both = jnp.concatenate([wk_ref[...], wv_ref[...]], axis=1)
    kv_ref[...] = (
        jnp.dot(encoded, w_both, preferred_element_type=jnp.float32)
        .astype(jnp.bfloat16)
        .reshape(pieces, GROUP * rows, 2 * width)
    )
    keys_total = pieces * rows
    group = range(GROUP)
    tokens = [slice(s * STRETCH, (s + 1) * STRETCH) for s in group]
    q2 = [block_diagonal(q_ref[tokens[s], :]) for s in group]
    g2 = [block_diagonal(g_ref[tokens[s], :]) for s in group]
    kv = [
        kv_ref[:, s * rows : (s + 1) * rows, :].reshape(keys_total, 2 * width) for s in group
    ]
    scores = [dot_nt(kv[s][:, :width], q2[s]) * score_scale for s in group]
    grad_probs = [dot_nt(kv[s][:, width:], g2[s]) for s in group]
    weights = [jnp.exp(x - jnp.max(x, axis=0, keepdims=True)) for x in scores]
    probs = [x * (1.0 / jnp.sum(x, axis=0, keepdims=True)) for x in weights]
    probs_low = [x.astype(jnp.bfloat16) for x in probs]
    inner = [jnp.sum(p * g, axis=0, keepdims=True) for p, g in zip(probs, grad_probs)]
    grad_scores = [
        (p * (g - i)).astype(jnp.bfloat16) for p, g, i in zip(probs, grad_probs, inner)
    ]
    for s in group:
        out2 = dot_tn(probs_low[s], kv[s][:, width:])
        att_ref[tokens[s], :] = jnp.concatenate(
            [out2[:STRETCH, :HEAD_DIM], out2[STRETCH:, HEAD_DIM:]], axis=1
        ).astype(jnp.bfloat16)
        cols = slice(s * keys_total, (s + 1) * keys_total)
        dkv_ref[:width, cols] = (dot_nt(q2[s].T, grad_scores[s]) * score_scale).astype(jnp.bfloat16)
        dkv_ref[width:, cols] = dot_nt(g2[s].T, probs_low[s]).astype(jnp.bfloat16)
    by_stretch = jnp.concatenate(
        [e[s * rows : (s + 1) * rows, :] for s in range(GROUP) for e in e_refs], axis=0
    )
    part = jnp.dot(dkv_ref[...], by_stretch, preferred_element_type=jnp.float32)

    @pl.when(step == 0)
    def _():
        acc_ref[...] = sum_ref[...] + part if last else part

    @pl.when(step > 0)
    def _():
        acc_ref[...] += part

    if last:

        @pl.when(step == pl.num_programs(0) - 1)
        def _():
            grad_ref[...] = acc_ref[...].T.astype(grad_ref.dtype)


def attend(queries, grad_out, w_key, w_value, encoded, half, earlier):
    tokens, width = queries.shape
    enc = w_key.shape[0]
    stretches = tokens // STRETCH // HALVES
    pieces = len(encoded)
    rows = encoded[0].shape[0] // stretches
    keys_total = pieces * rows
    steps = stretches // GROUP
    last = half == HALVES - 1
    token_block = pl.BlockSpec((GROUP * STRETCH, width), lambda i: (half * steps + i, 0))
    whole_w = pl.BlockSpec((enc, width), lambda i: (0, 0))
    sum_block = pl.BlockSpec((2 * width, enc), lambda i: (0, 0))
    sum_shape = jax.ShapeDtypeStruct((2 * width, enc), jnp.float32)
    piece_block = pl.BlockSpec((GROUP * rows, enc), lambda i: (i, 0))
    flops = 2 * stretches * keys_total * enc * 4 * width + 5 * tokens * keys_total * width
    scratch = [
        pltpu.VMEM((pieces, GROUP * rows, 2 * width), jnp.bfloat16),
        pltpu.VMEM((2 * width, GROUP * keys_total), jnp.bfloat16),
    ]
    in_specs = [token_block, token_block, whole_w, whole_w] + [piece_block] * pieces
    att_shape = jax.ShapeDtypeStruct((tokens, width), jnp.bfloat16)
    if last:
        in_specs += [sum_block, pl.BlockSpec(memory_space=pl.ANY)]
        out_specs = [token_block, pl.BlockSpec((enc, 2 * width), lambda i: (0, 0))]
        out_shape = [att_shape, jax.ShapeDtypeStruct((enc, 2 * width), jnp.bfloat16)]
        scratch.append(pltpu.VMEM(sum_shape.shape, sum_shape.dtype))
        aliases = {5 + pieces: 0}
    else:
        out_specs = [token_block, sum_block]
        out_shape = [att_shape, sum_shape]
        aliases = {}
    return pl.pallas_call(
        functools.partial(attention_kernel, pieces=pieces, rows=rows, last=last),
        grid=(steps,),
        in_specs=in_specs,
        out_specs=out_specs,
        out_shape=out_shape,
        scratch_shapes=scratch,
        input_output_aliases=aliases,
        cost_estimate=pl.CostEstimate(
            flops=flops, bytes_accessed=6_000_000, transcendentals=500_000
        ),
        compiler_params=pltpu.CompilerParams(vmem_limit_bytes=40 * 1024 * 1024),
        name="attention",
    )(queries, grad_out, w_key, w_value, *encoded, *earlier)


def pick_kernel(index_ref, source_ref, *refs):
    *outs, sem = refs
    for half, out_ref in enumerate(outs):
        count = out_ref.shape[0]

        @pl.loop(0, count)
        def _(i):
            row = source_ref.at[index_ref[half * count + i]]
            pltpu.make_async_copy(row, out_ref.at[i], sem.at[half]).start()

    for half, out_ref in enumerate(outs):
        pltpu.make_async_copy(out_ref, out_ref, sem.at[half]).wait()


def pick(source, index):
    count = index.shape[0] // HALVES
    rows, width = source.shape[1:]
    return pl.pallas_call(
        pick_kernel,
        grid_spec=pltpu.PrefetchScalarGridSpec(
            num_scalar_prefetch=1,
            grid=(),
            in_specs=[pl.BlockSpec(memory_space=pl.ANY)],
            out_specs=[pl.BlockSpec(memory_space=pl.ANY)] * HALVES,
            scratch_shapes=[pltpu.SemaphoreType.DMA((HALVES,))],
        ),
        out_shape=[jax.ShapeDtypeStruct((count, rows, width), source.dtype)] * HALVES,
        cost_estimate=pl.CostEstimate(
            flops=0, bytes_accessed=8 * count * rows * width, transcendentals=0
        ),
        compiler_params=pltpu.CompilerParams(vmem_limit_bytes=1024 * 1024),
        name="pick",
    )(index, source)


def request_kernel(owner_ref, id_ref, wanted_ref, own_ref):
    groups, lanes = wanted_ref.shape
    slots = owner_ref.shape[1]
    owners = owner_ref[...]
    ids = id_ref[...].astype(jnp.float32)
    match = lax.broadcasted_iota(jnp.int32, (groups, slots), 0) == owners
    row = lax.broadcasted_iota(jnp.int32, (slots, slots), 0)
    col = lax.broadcasted_iota(jnp.int32, (slots, slots), 1)
    rank = jnp.dot(
        match.astype(jnp.bfloat16),
        (row < col).astype(jnp.bfloat16),
        preferred_element_type=jnp.float32,
    )
    lane = lax.broadcasted_iota(jnp.int32, (groups, lanes), 1)
    wanted = jnp.zeros((groups, lanes), jnp.float32)
    for turn in range(MOST):
        asked = jnp.where(match & (rank == turn), ids, 0.0)
        wanted = jnp.where(lane == turn, jnp.sum(asked, axis=1, keepdims=True), wanted)
    wanted_ref[...] = wanted.astype(jnp.int32)
    own_rank = jnp.sum(jnp.where(match, rank, 0.0), axis=0, keepdims=True)
    own_ref[...] = owners * MOST + own_rank.astype(jnp.int32)


def requests(owner, local_id, groups):
    slots = owner.shape[0]
    return pl.pallas_call(
        request_kernel,
        out_shape=[
            jax.ShapeDtypeStruct((groups, 128), jnp.int32),
            jax.ShapeDtypeStruct((1, slots), jnp.int32),
        ],
        name="requests",
    )(owner.reshape(1, slots), local_id.reshape(1, slots))


def exchange(x):
    return lax.all_to_all(x, "dp", split_axis=0, concat_axis=0, tiled=True)


def ring_gather(x, far_right):
    size = lax.axis_size("head")
    rightward = [(i, (i + 1) % size) for i in range(size)]
    leftward = [(i, (i - 1) % size) for i in range(size)]
    pieces = [x]
    right = left = x
    for _ in range((size - 1) // 2):
        right = lax.ppermute(right, "head", rightward)
        left = lax.ppermute(left, "head", leftward)
        pieces += [right, left]
    if far_right:
        pieces.append(lax.ppermute(right, "head", rightward))
    else:
        pieces.append(lax.ppermute(left, "head", leftward))
    return pieces


def per_device(queries, table, owner, local_id, w_key, w_value, grad_out):
    groups = lax.axis_size("dp")
    slot_count = owner.shape[0]
    wanted, own_index = requests(owner, local_id, groups)
    asked_ids = exchange(wanted)[:, :MOST].reshape(-1)
    own_index = own_index.reshape(slot_count)
    part, enc_width = table.shape[1:]
    replies = jnp.take(table, asked_ids, axis=0, mode="clip")
    fetched = exchange(replies.reshape(groups, MOST, part, enc_width))
    fetched = fetched.reshape(groups * MOST, part, enc_width)
    queries, grad_out, w_key, w_value = (
        pltpu.with_memory_space_constraint(x, pltpu.HBM)
        for x in (queries, grad_out, w_key, w_value)
    )
    own = pick(fetched, own_index)
    results = ()
    for half in range(HALVES):
        pieces = ring_gather(own[half].reshape(-1, enc_width), half % 2 == 0)
        pieces[:EARLY] = [
            pltpu.with_memory_space_constraint(piece, pltpu.HBM) for piece in pieces[:EARLY]
        ]
        results = attend(queries, grad_out, w_key, w_value, pieces, half, results[::-1])
    attended, grads = results
    width = w_key.shape[1]
    share = enc_width // groups
    lanes = 2 * width // 128
    sent = grads.reshape(groups // CORES, CORES, share, lanes, 128).transpose(1, 0, 3, 2, 4)
    sent = sent.reshape(CORES, groups // CORES, lanes * share, 128)
    core = lax.axis_index("dp") % CORES
    mine = lax.dynamic_index_in_dim(sent, core, 0, keepdims=False)
    partner = lax.dynamic_index_in_dim(sent, 1 - core, 0, keepdims=False)
    swap = [(i, i ^ 1) for i in range(groups)]
    both = mine.astype(jnp.float32) + lax.ppermute(partner, "dp", swap).astype(jnp.float32)
    same_core = [list(range(c, groups, CORES)) for c in range(CORES)]
    terms = lax.all_to_all(
        both.astype(jnp.bfloat16),
        "dp",
        split_axis=0,
        concat_axis=0,
        axis_index_groups=same_core,
        tiled=True,
    )
    total = jnp.sum(terms.astype(jnp.float32), axis=0).reshape(lanes, share, 128)
    total = total.transpose(1, 0, 2).reshape(share, 2 * width)
    return attended, total[:, :width], total[:, width:]


def solution(mesh):
    in_specs = (
        P("dp", "head"),
        P("dp", "head", None),
        P("dp", None),
        P("dp", None),
        P(None, "head"),
        P(None, "head"),
        P("dp", "head"),
    )
    out_specs = (P("dp", "head"), P("dp", "head"), P("dp", "head"))
    return jax.shard_map(
        per_device, mesh=mesh, in_specs=in_specs, out_specs=out_specs, check_vma=False
    )
```

```python
import functools

import jax
import jax.numpy as jnp
from jax import lax
from jax.experimental import pallas as pl
from jax.experimental.pallas import tpu as pltpu
from jax.sharding import PartitionSpec as P

HEAD_DIM = 128
STRETCH = 64
MOST = 2
HALVES = 2
CORES = 2
GROUP = 8
EARLY = 3


def block_diagonal(rows):
    left, right = rows[:, :HEAD_DIM], rows[:, HEAD_DIM:]
    zero = jnp.zeros_like(left)
    return jnp.concatenate(
        [jnp.concatenate([left, zero], axis=1), jnp.concatenate([zero, right], axis=1)], axis=0
    )


def dot_nt(a, b):
    return lax.dot_general(a, b, (((1,), (1,)), ((), ())), preferred_element_type=jnp.float32)


def dot_tn(a, b):
    return lax.dot_general(a, b, (((0,), (0,)), ((), ())), preferred_element_type=jnp.float32)


def attention_kernel(*refs, pieces, rows, last):
    q_ref, g_ref, wk_ref, wv_ref = refs[:4]
    e_refs = refs[4 : 4 + pieces]
    if last:
        sum_ref, _, att_ref, grad_ref, kv_ref, dkv_ref, acc_ref, sem = refs[4 + pieces :]
        earlier_sum = pltpu.make_async_copy(sum_ref, acc_ref, sem)
        earlier_sum.start()
    else:
        att_ref, acc_ref, kv_ref, dkv_ref = refs[4 + pieces :]
    width = wk_ref.shape[1]
    score_scale = HEAD_DIM ** (-0.5)
    encoded = jnp.concatenate([e[...] for e in e_refs], axis=0)
    w_both = jnp.concatenate([wk_ref[...], wv_ref[...]], axis=1)
    kv_ref[...] = (
        jnp.dot(encoded, w_both, preferred_element_type=jnp.float32)
        .astype(jnp.bfloat16)
        .reshape(pieces, GROUP * rows, 2 * width)
    )
    keys_total = pieces * rows
    group = range(GROUP)
    tokens = [slice(s * STRETCH, (s + 1) * STRETCH) for s in group]
    q2 = [block_diagonal(q_ref[tokens[s], :]) for s in group]
    g2 = [block_diagonal(g_ref[tokens[s], :]) for s in group]
    kv = [
        kv_ref[:, s * rows : (s + 1) * rows, :].reshape(keys_total, 2 * width) for s in group
    ]
    scores = [dot_nt(kv[s][:, :width], q2[s]) * score_scale for s in group]
    grad_probs = [dot_nt(kv[s][:, width:], g2[s]) for s in group]
    weights = [jnp.exp(x - jnp.max(x, axis=0, keepdims=True)) for x in scores]
    probs = [x * (1.0 / jnp.sum(x, axis=0, keepdims=True)) for x in weights]
    probs_low = [x.astype(jnp.bfloat16) for x in probs]
    inner = [jnp.sum(p * g, axis=0, keepdims=True) for p, g in zip(probs, grad_probs)]
    grad_scores = [
        (p * (g - i)).astype(jnp.bfloat16) for p, g, i in zip(probs, grad_probs, inner)
    ]
    for s in group:
        out2 = dot_tn(probs_low[s], kv[s][:, width:])
        att_ref[tokens[s], :] = jnp.concatenate(
            [out2[:STRETCH, :HEAD_DIM], out2[STRETCH:, HEAD_DIM:]], axis=1
        ).astype(jnp.bfloat16)
        cols = slice(s * keys_total, (s + 1) * keys_total)
        dkv_ref[:width, cols] = (dot_nt(q2[s].T, grad_scores[s]) * score_scale).astype(jnp.bfloat16)
        dkv_ref[width:, cols] = dot_nt(g2[s].T, probs_low[s]).astype(jnp.bfloat16)
    by_stretch = jnp.concatenate(
        [e[s * rows : (s + 1) * rows, :] for s in range(GROUP) for e in e_refs], axis=0
    )
    part = jnp.dot(dkv_ref[...], by_stretch, preferred_element_type=jnp.float32)

    if last:
        earlier_sum.wait()
        grad_ref[...] = (acc_ref[...] + part).T.astype(grad_ref.dtype)
    else:
        acc_ref[...] = part


def attend(queries, grad_out, w_key, w_value, encoded, half, earlier):
    tokens, width = queries.shape
    enc = w_key.shape[0]
    stretches = tokens // STRETCH // HALVES
    pieces = len(encoded)
    rows = encoded[0].shape[0] // stretches
    keys_total = pieces * rows
    steps = stretches // GROUP
    last = half == HALVES - 1
    token_block = pl.BlockSpec((GROUP * STRETCH, width), lambda i: (half * steps + i, 0))
    whole_w = pl.BlockSpec((enc, width), lambda i: (0, 0))
    sum_block = pl.BlockSpec((2 * width, enc), lambda i: (0, 0))
    sum_shape = jax.ShapeDtypeStruct((2 * width, enc), jnp.float32)
    piece_block = pl.BlockSpec((GROUP * rows, enc), lambda i: (i, 0))
    flops = 2 * stretches * keys_total * enc * 4 * width + 5 * tokens * keys_total * width
    scratch = [
        pltpu.VMEM((pieces, GROUP * rows, 2 * width), jnp.bfloat16),
        pltpu.VMEM((2 * width, GROUP * keys_total), jnp.bfloat16),
    ]
    in_specs = [token_block, token_block, whole_w, whole_w] + [piece_block] * pieces
    att_shape = jax.ShapeDtypeStruct((tokens, width), jnp.bfloat16)
    if last:
        in_specs += [pl.BlockSpec(memory_space=pl.ANY)] * 2
        out_specs = [token_block, pl.BlockSpec((enc, 2 * width), lambda i: (0, 0))]
        out_shape = [att_shape, jax.ShapeDtypeStruct((enc, 2 * width), jnp.bfloat16)]
        scratch += [pltpu.VMEM(sum_shape.shape, sum_shape.dtype), pltpu.SemaphoreType.DMA]
        aliases = {5 + pieces: 0}
    else:
        out_specs = [token_block, sum_block]
        out_shape = [att_shape, sum_shape]
        aliases = {}
    return pl.pallas_call(
        functools.partial(attention_kernel, pieces=pieces, rows=rows, last=last),
        grid=(steps,),
        in_specs=in_specs,
        out_specs=out_specs,
        out_shape=out_shape,
        scratch_shapes=scratch,
        input_output_aliases=aliases,
        cost_estimate=pl.CostEstimate(
            flops=flops, bytes_accessed=6_000_000, transcendentals=500_000
        ),
        compiler_params=pltpu.CompilerParams(vmem_limit_bytes=40 * 1024 * 1024),
        name="attention",
    )(queries, grad_out, w_key, w_value, *encoded, *earlier)


def pick_kernel(index_ref, source_ref, *refs):
    *outs, sem = refs
    for half, out_ref in enumerate(outs):
        count = out_ref.shape[0]

        @pl.loop(0, count)
        def _(i):
            row = source_ref.at[index_ref[half * count + i]]
            pltpu.make_async_copy(row, out_ref.at[i], sem.at[half]).start()

    for half, out_ref in enumerate(outs):
        pltpu.make_async_copy(out_ref, out_ref, sem.at[half]).wait()


def pick(source, index):
    count = index.shape[0] // HALVES
    rows, width = source.shape[1:]
    return pl.pallas_call(
        pick_kernel,
        grid_spec=pltpu.PrefetchScalarGridSpec(
            num_scalar_prefetch=1,
            grid=(),
            in_specs=[pl.BlockSpec(memory_space=pl.ANY)],
            out_specs=[pl.BlockSpec(memory_space=pl.ANY)] * HALVES,
            scratch_shapes=[pltpu.SemaphoreType.DMA((HALVES,))],
        ),
        out_shape=[jax.ShapeDtypeStruct((count, rows, width), source.dtype)] * HALVES,
        cost_estimate=pl.CostEstimate(
            flops=0, bytes_accessed=8 * count * rows * width, transcendentals=0
        ),
        compiler_params=pltpu.CompilerParams(vmem_limit_bytes=1024 * 1024),
        name="pick",
    )(index, source)


def request_kernel(owner_ref, id_ref, wanted_ref, own_ref):
    groups, lanes = wanted_ref.shape
    slots = owner_ref.shape[1]
    owners = owner_ref[...]
    ids = id_ref[...].astype(jnp.float32)
    match = lax.broadcasted_iota(jnp.int32, (groups, slots), 0) == owners
    row = lax.broadcasted_iota(jnp.int32, (slots, slots), 0)
    col = lax.broadcasted_iota(jnp.int32, (slots, slots), 1)
    rank = jnp.dot(
        match.astype(jnp.bfloat16),
        (row < col).astype(jnp.bfloat16),
        preferred_element_type=jnp.float32,
    )
    lane = lax.broadcasted_iota(jnp.int32, (groups, lanes), 1)
    wanted = jnp.zeros((groups, lanes), jnp.float32)
    for turn in range(MOST):
        asked = jnp.where(match & (rank == turn), ids, 0.0)
        wanted = jnp.where(lane == turn, jnp.sum(asked, axis=1, keepdims=True), wanted)
    wanted_ref[...] = wanted.astype(jnp.int32)
    own_rank = jnp.sum(jnp.where(match, rank, 0.0), axis=0, keepdims=True)
    own_ref[...] = owners * MOST + own_rank.astype(jnp.int32)


def requests(owner, local_id, groups):
    slots = owner.shape[0]
    return pl.pallas_call(
        request_kernel,
        out_shape=[
            jax.ShapeDtypeStruct((groups, 128), jnp.int32),
            jax.ShapeDtypeStruct((1, slots), jnp.int32),
        ],
        name="requests",
    )(owner.reshape(1, slots), local_id.reshape(1, slots))


def exchange(x):
    return lax.all_to_all(x, "dp", split_axis=0, concat_axis=0, tiled=True)


def ring_gather(x, far_right):
    size = lax.axis_size("head")
    rightward = [(i, (i + 1) % size) for i in range(size)]
    leftward = [(i, (i - 1) % size) for i in range(size)]
    pieces = [x]
    right = left = x
    for _ in range((size - 1) // 2):
        right = lax.ppermute(right, "head", rightward)
        left = lax.ppermute(left, "head", leftward)
        pieces += [right, left]
    if far_right:
        pieces.append(lax.ppermute(right, "head", rightward))
    else:
        pieces.append(lax.ppermute(left, "head", leftward))
    return pieces


def per_device(queries, table, owner, local_id, w_key, w_value, grad_out):
    groups = lax.axis_size("dp")
    slot_count = owner.shape[0]
    wanted, own_index = requests(owner, local_id, groups)
    asked_ids = exchange(wanted)[:, :MOST].reshape(-1)
    own_index = own_index.reshape(slot_count)
    part, enc_width = table.shape[1:]
    replies = jnp.take(table, asked_ids, axis=0, mode="clip")
    fetched = exchange(replies.reshape(groups, MOST, part, enc_width))
    fetched = fetched.reshape(groups * MOST, part, enc_width)
    queries, grad_out, w_key, w_value = (
        pltpu.with_memory_space_constraint(x, pltpu.HBM)
        for x in (queries, grad_out, w_key, w_value)
    )
    own = pick(fetched, own_index)
    results = ()
    for half in range(HALVES):
        pieces = ring_gather(own[half].reshape(-1, enc_width), half % 2 == 0)
        pieces[:EARLY] = [
            pltpu.with_memory_space_constraint(piece, pltpu.HBM) for piece in pieces[:EARLY]
        ]
        results = attend(queries, grad_out, w_key, w_value, pieces, half, results[::-1])
    attended, grads = results
    width = w_key.shape[1]
    share = enc_width // groups
    lanes = 2 * width // 128
    sent = grads.reshape(groups // CORES, CORES, share, lanes, 128).transpose(1, 0, 3, 2, 4)
    sent = sent.reshape(CORES, groups // CORES, lanes * share, 128)
    core = lax.axis_index("dp") % CORES
    mine = lax.dynamic_index_in_dim(sent, core, 0, keepdims=False)
    partner = lax.dynamic_index_in_dim(sent, 1 - core, 0, keepdims=False)
    swap = [(i, i ^ 1) for i in range(groups)]
    both = mine.astype(jnp.float32) + lax.ppermute(partner, "dp", swap).astype(jnp.float32)
    same_core = [list(range(c, groups, CORES)) for c in range(CORES)]
    terms = lax.all_to_all(
        both.astype(jnp.bfloat16),
        "dp",
        split_axis=0,
        concat_axis=0,
        axis_index_groups=same_core,
        tiled=True,
    )
    total = jnp.sum(terms.astype(jnp.float32), axis=0).reshape(lanes, share, 128)
    total = total.transpose(1, 0, 2).reshape(share, 2 * width)
    return attended, total[:, :width], total[:, width:]


def solution(mesh):
    in_specs = (
        P("dp", "head"),
        P("dp", "head", None),
        P("dp", None),
        P("dp", None),
        P(None, "head"),
        P(None, "head"),
        P("dp", "head"),
    )
    out_specs = (P("dp", "head"), P("dp", "head"), P("dp", "head"))
    return jax.shard_map(
        per_device, mesh=mesh, in_specs=in_specs, out_specs=out_specs, check_vma=False
    )
```

```python
import functools

import jax
import jax.numpy as jnp
from jax import lax
from jax.experimental import pallas as pl
from jax.experimental.pallas import tpu as pltpu
from jax.sharding import PartitionSpec as P

HEAD_DIM = 128
STRETCH = 64
MOST = 2
HALVES = 2
CORES = 2
GROUP = 8
EARLY = 5


def block_diagonal(rows):
    left, right = rows[:, :HEAD_DIM], rows[:, HEAD_DIM:]
    zero = jnp.zeros_like(left)
    return jnp.concatenate(
        [jnp.concatenate([left, zero], axis=1), jnp.concatenate([zero, right], axis=1)], axis=0
    )


def dot_nt(a, b):
    return lax.dot_general(a, b, (((1,), (1,)), ((), ())), preferred_element_type=jnp.float32)


def dot_tn(a, b):
    return lax.dot_general(a, b, (((0,), (0,)), ((), ())), preferred_element_type=jnp.float32)


def attention_kernel(*refs, pieces, rows, last):
    q_ref, g_ref, wk_ref, wv_ref = refs[:4]
    e_refs = refs[4 : 4 + pieces]
    if last:
        sum_ref, _, att_ref, grad_ref, kv_ref, dkv_ref, acc_ref = refs[4 + pieces :]
    else:
        att_ref, acc_ref, kv_ref, dkv_ref = refs[4 + pieces :]
    step = pl.program_id(0)
    width = wk_ref.shape[1]
    score_scale = HEAD_DIM ** (-0.5)
    encoded = jnp.concatenate([e[...] for e in e_refs], axis=0)
    w_both = jnp.concatenate([wk_ref[...], wv_ref[...]], axis=1)
    kv_ref[...] = (
        jnp.dot(encoded, w_both, preferred_element_type=jnp.float32)
        .astype(jnp.bfloat16)
        .reshape(pieces, GROUP * rows, 2 * width)
    )
    keys_total = pieces * rows
    group = range(GROUP)
    tokens = [slice(s * STRETCH, (s + 1) * STRETCH) for s in group]
    q2 = [block_diagonal(q_ref[tokens[s], :]) for s in group]
    g2 = [block_diagonal(g_ref[tokens[s], :]) for s in group]
    kv = [
        kv_ref[:, s * rows : (s + 1) * rows, :].reshape(keys_total, 2 * width) for s in group
    ]
    scores = [dot_nt(kv[s][:, :width], q2[s]) * score_scale for s in group]
    grad_probs = [dot_nt(kv[s][:, width:], g2[s]) for s in group]
    weights = [jnp.exp(x - jnp.max(x, axis=0, keepdims=True)) for x in scores]
    probs = [x * (1.0 / jnp.sum(x, axis=0, keepdims=True)) for x in weights]
    probs_low = [x.astype(jnp.bfloat16) for x in probs]
    inner = [jnp.sum(p * g, axis=0, keepdims=True) for p, g in zip(probs, grad_probs)]
    grad_scores = [
        (p * (g - i)).astype(jnp.bfloat16) for p, g, i in zip(probs, grad_probs, inner)
    ]
    for s in group:
        out2 = dot_tn(probs_low[s], kv[s][:, width:])
        att_ref[tokens[s], :] = jnp.concatenate(
            [out2[:STRETCH, :HEAD_DIM], out2[STRETCH:, HEAD_DIM:]], axis=1
        ).astype(jnp.bfloat16)
        cols = slice(s * keys_total, (s + 1) * keys_total)
        dkv_ref[:width, cols] = (dot_nt(q2[s].T, grad_scores[s]) * score_scale).astype(jnp.bfloat16)
        dkv_ref[width:, cols] = dot_nt(g2[s].T, probs_low[s]).astype(jnp.bfloat16)
    by_stretch = jnp.concatenate(
        [e[s * rows : (s + 1) * rows, :] for s in range(GROUP) for e in e_refs], axis=0
    )
    part = jnp.dot(dkv_ref[...], by_stretch, preferred_element_type=jnp.float32)

    @pl.when(step == 0)
    def _():
        acc_ref[...] = sum_ref[...] + part if last else part

    @pl.when(step > 0)
    def _():
        acc_ref[...] += part

    if last:

        @pl.when(step == pl.num_programs(0) - 1)
        def _():
            grad_ref[...] = acc_ref[...].astype(grad_ref.dtype).T


def attend(queries, grad_out, w_key, w_value, encoded, half, earlier):
    tokens, width = queries.shape
    enc = w_key.shape[0]
    stretches = tokens // STRETCH // HALVES
    pieces = len(encoded)
    rows = encoded[0].shape[0] // stretches
    keys_total = pieces * rows
    steps = stretches // GROUP
    last = half == HALVES - 1
    token_block = pl.BlockSpec((GROUP * STRETCH, width), lambda i: (half * steps + i, 0))
    whole_w = pl.BlockSpec((enc, width), lambda i: (0, 0))
    sum_block = pl.BlockSpec((2 * width, enc), lambda i: (0, 0))
    sum_shape = jax.ShapeDtypeStruct((2 * width, enc), jnp.float32)
    piece_block = pl.BlockSpec((GROUP * rows, enc), lambda i: (i, 0))
    flops = 2 * stretches * keys_total * enc * 4 * width + 5 * tokens * keys_total * width
    scratch = [
        pltpu.VMEM((pieces, GROUP * rows, 2 * width), jnp.bfloat16),
        pltpu.VMEM((2 * width, GROUP * keys_total), jnp.bfloat16),
    ]
    in_specs = [token_block, token_block, whole_w, whole_w] + [piece_block] * pieces
    att_shape = jax.ShapeDtypeStruct((tokens, width), jnp.bfloat16)
    if last:
        in_specs += [sum_block, pl.BlockSpec(memory_space=pl.ANY)]
        out_specs = [token_block, pl.BlockSpec((enc, 2 * width), lambda i: (0, 0))]
        out_shape = [att_shape, jax.ShapeDtypeStruct((enc, 2 * width), jnp.bfloat16)]
        scratch.append(pltpu.VMEM(sum_shape.shape, sum_shape.dtype))
        aliases = {5 + pieces: 0}
    else:
        out_specs = [token_block, sum_block]
        out_shape = [att_shape, sum_shape]
        aliases = {}
    return pl.pallas_call(
        functools.partial(attention_kernel, pieces=pieces, rows=rows, last=last),
        grid=(steps,),
        in_specs=in_specs,
        out_specs=out_specs,
        out_shape=out_shape,
        scratch_shapes=scratch,
        input_output_aliases=aliases,
        cost_estimate=pl.CostEstimate(
            flops=flops, bytes_accessed=6_000_000, transcendentals=500_000
        ),
        compiler_params=pltpu.CompilerParams(vmem_limit_bytes=40 * 1024 * 1024),
        name="attention",
    )(queries, grad_out, w_key, w_value, *encoded, *earlier)


def pick_kernel(index_ref, source_ref, *refs):
    *outs, sem = refs
    for half, out_ref in enumerate(outs):
        count = out_ref.shape[0]

        @pl.loop(0, count)
        def _(i):
            row = source_ref.at[index_ref[half * count + i]]
            pltpu.make_async_copy(row, out_ref.at[i], sem.at[half]).start()

    for half, out_ref in enumerate(outs):
        pltpu.make_async_copy(out_ref, out_ref, sem.at[half]).wait()


def pick(source, index):
    count = index.shape[0] // HALVES
    rows, width = source.shape[1:]
    return pl.pallas_call(
        pick_kernel,
        grid_spec=pltpu.PrefetchScalarGridSpec(
            num_scalar_prefetch=1,
            grid=(),
            in_specs=[pl.BlockSpec(memory_space=pl.ANY)],
            out_specs=[pl.BlockSpec(memory_space=pl.ANY)] * HALVES,
            scratch_shapes=[pltpu.SemaphoreType.DMA((HALVES,))],
        ),
        out_shape=[jax.ShapeDtypeStruct((count, rows, width), source.dtype)] * HALVES,
        cost_estimate=pl.CostEstimate(
            flops=0, bytes_accessed=8 * count * rows * width, transcendentals=0
        ),
        compiler_params=pltpu.CompilerParams(vmem_limit_bytes=1024 * 1024),
        name="pick",
    )(index, source)


def request_kernel(owner_ref, id_ref, wanted_ref, own_ref):
    groups, lanes = wanted_ref.shape
    slots = owner_ref.shape[1]
    owners = owner_ref[...]
    ids = id_ref[...].astype(jnp.float32)
    match = lax.broadcasted_iota(jnp.int32, (groups, slots), 0) == owners
    row = lax.broadcasted_iota(jnp.int32, (slots, slots), 0)
    col = lax.broadcasted_iota(jnp.int32, (slots, slots), 1)
    rank = jnp.dot(
        match.astype(jnp.bfloat16),
        (row < col).astype(jnp.bfloat16),
        preferred_element_type=jnp.float32,
    )
    lane = lax.broadcasted_iota(jnp.int32, (groups, lanes), 1)
    wanted = jnp.zeros((groups, lanes), jnp.float32)
    for turn in range(MOST):
        asked = jnp.where(match & (rank == turn), ids, 0.0)
        wanted = jnp.where(lane == turn, jnp.sum(asked, axis=1, keepdims=True), wanted)
    wanted_ref[...] = wanted.astype(jnp.int32)
    own_rank = jnp.sum(jnp.where(match, rank, 0.0), axis=0, keepdims=True)
    own_ref[...] = owners * MOST + own_rank.astype(jnp.int32)


def requests(owner, local_id, groups):
    slots = owner.shape[0]
    return pl.pallas_call(
        request_kernel,
        out_shape=[
            jax.ShapeDtypeStruct((groups, 128), jnp.int32),
            jax.ShapeDtypeStruct((1, slots), jnp.int32),
        ],
        name="requests",
    )(owner.reshape(1, slots), local_id.reshape(1, slots))


def exchange(x):
    return lax.all_to_all(x, "dp", split_axis=0, concat_axis=0, tiled=True)


def ring_gather(x, far_right):
    size = lax.axis_size("head")
    rightward = [(i, (i + 1) % size) for i in range(size)]
    leftward = [(i, (i - 1) % size) for i in range(size)]
    pieces = [x]
    right = left = x
    for _ in range((size - 1) // 2):
        right = lax.ppermute(right, "head", rightward)
        left = lax.ppermute(left, "head", leftward)
        pieces += [right, left]
    if far_right:
        pieces.append(lax.ppermute(right, "head", rightward))
    else:
        pieces.append(lax.ppermute(left, "head", leftward))
    return pieces


def per_device(queries, table, owner, local_id, w_key, w_value, grad_out):
    groups = lax.axis_size("dp")
    slot_count = owner.shape[0]
    wanted, own_index = requests(owner, local_id, groups)
    asked_ids = exchange(wanted)[:, :MOST].reshape(-1)
    own_index = own_index.reshape(slot_count)
    part, enc_width = table.shape[1:]
    replies = jnp.take(table, asked_ids, axis=0, mode="clip")
    fetched = exchange(replies.reshape(groups, MOST, part, enc_width))
    fetched = fetched.reshape(groups * MOST, part, enc_width)
    queries, grad_out, w_key, w_value = (
        pltpu.with_memory_space_constraint(x, pltpu.HBM)
        for x in (queries, grad_out, w_key, w_value)
    )
    own = pick(fetched, own_index)
    results = ()
    for half in range(HALVES):
        pieces = ring_gather(own[half].reshape(-1, enc_width), half % 2 == 0)
        pieces[:EARLY] = [
            pltpu.with_memory_space_constraint(piece, pltpu.HBM) for piece in pieces[:EARLY]
        ]
        results = attend(queries, grad_out, w_key, w_value, pieces, half, results[::-1])
    attended, grads = results
    width = w_key.shape[1]
    share = enc_width // groups
    lanes = 2 * width // 128
    sent = grads.reshape(groups // CORES, CORES, share, lanes, 128).transpose(1, 0, 3, 2, 4)
    sent = sent.reshape(CORES, groups // CORES, lanes * share, 128)
    core = lax.axis_index("dp") % CORES
    mine = lax.dynamic_index_in_dim(sent, core, 0, keepdims=False)
    partner = lax.dynamic_index_in_dim(sent, 1 - core, 0, keepdims=False)
    swap = [(i, i ^ 1) for i in range(groups)]
    both = mine.astype(jnp.float32) + lax.ppermute(partner, "dp", swap).astype(jnp.float32)
    same_core = [list(range(c, groups, CORES)) for c in range(CORES)]
    terms = lax.all_to_all(
        both.astype(jnp.bfloat16),
        "dp",
        split_axis=0,
        concat_axis=0,
        axis_index_groups=same_core,
        tiled=True,
    )
    total = jnp.sum(terms.astype(jnp.float32), axis=0).reshape(lanes, share, 128)
    total = total.transpose(1, 0, 2).reshape(share, 2 * width)
    return attended, total[:, :width], total[:, width:]


def solution(mesh):
    in_specs = (
        P("dp", "head"),
        P("dp", "head", None),
        P("dp", None),
        P("dp", None),
        P(None, "head"),
        P(None, "head"),
        P("dp", "head"),
    )
    out_specs = (P("dp", "head"), P("dp", "head"), P("dp", "head"))
    return jax.shard_map(
        per_device, mesh=mesh, in_specs=in_specs, out_specs=out_specs, check_vma=False
    )
```
